32 devices in a mesh: ens: 2 (over y), gx: 16 (over z, x, core).
Axes of the slice: x: 2, y: 2, z: 4, core: 2. Of those that a mesh axis runs over, the one named last changes fastest.
Arguments:
- pressure_prev: float32 [8, 128, 128], P('ens', 'gx'), parts along dimension 0, may hold values from -2.5 to 2.5
- source: float32 [8, 128, 128], P('ens', 'gx'), parts along dimension 0, may hold values from -8 to 8
- permeability: float32 [8, 128, 128], P('ens', 'gx'), parts along dimension 0, may hold values from 0.3 to 3
- region: int32 [8, 128, 128], P('ens', 'gx'), parts along dimension 0, may hold values from 0 to 7
- region_factor: float32 [16], P('ens'), parts along dimension 0, may hold values from 0.3 to 3
- boundary: int32 [8, 128, 128], P('ens', 'gx'), parts along dimension 0, may hold values from 0 to 2
- flux_prev: float32 [3, 8, 128, 128], P(None, 'ens', 'gx'), parts along dimension 1, may hold values from -2 to 2
- concentration: float32 [4, 8, 128, 128], P(None, 'ens', 'gx'), parts along dimension 1, may hold values from 0.2 to 2
- porosity: float32 [8, 128, 128], P('ens', 'gx'), parts along dimension 0, may hold values from 0.3 to 1
- reaction: float32 [8, 4], P('ens'), parts along dimension 0, may hold values from -3 to 3
Outputs:
- pressure: float32 [8, 128, 128], P('ens', 'gx'), parts along dimension 0
- flux_new: float32 [3, 8, 128, 128], P(None, 'ens', 'gx'), parts along dimension 1
- species_new: float32 [4, 8, 128, 128], P(None, 'ens', 'gx'), parts along dimension 1
The draws below stay inside these ranges and needn't reach their ends.
There are 2 independent parts, one for each index of `ens`. The reference program is written for one: setup_inputs(seed, part) draws one part's arguments, and reference() takes and returns one part's arrays. A program takes and returns all parts, laid end to end along the dimension named above; each array names one. Nothing has to cross between parts.
Inputs may be any that keep to these rules, and one draw needn't show every extreme that they name: Index of the cell's material region into region_factor. 0 inner cell, 1 leaky boundary cell, 2 fixed-pressure well cell.
All inputs are finite; a program needn't handle non-finite values.
Results may differ from the reference program's by a relative error of at most 0.0003.
Values sent between devices are 32-bit elements; how exact they have to be, the bound alone decides.
No kernel may reach another device: no remote copies, remote signals or barrier semaphores. Data moves between devices by JAX's collectives and lax.ppermute only.
A program may use at most 64 MiB of HBM per device.

```python
import math
import jax
import jax.numpy as jnp
from jax import lax

LAYERS = 4
SPECIES = 4
REGIONS = 8
ITERS = 2
SUBSTEPS = 2
NX = 128
NY = 128


def draw_source(key, part):
    position = jnp.arange(NX, dtype=jnp.float32) / max(NX - 1, 1)
    rising = (1.0 + 2.0 * position)[None, :, None]
    values = jax.random.normal(key, (LAYERS, NX, NY), jnp.float32) * rising
    return jnp.clip(values, -8.0, 8.0)


def place_ends(drawn, rng, smallest, high):
    longest = drawn.shape.index(max(drawn.shape))
    spots = []
    for shift in (0, 1):
        where = [jax.random.randint(jax.random.fold_in(rng, axis), (), 0, length) for axis, length in enumerate(drawn.shape)]
        where[longest] = (where[longest] + shift) % drawn.shape[longest]
        spots.append(tuple(where))
    return drawn.at[spots[0]].set(smallest).at[spots[1]].set(high)


def block_scale(rng, dims, pieces, smallest, high):
    factor_of = 1.0
    for dim, blocks in pieces:
        draws = jax.random.uniform(jax.random.fold_in(jax.random.fold_in(rng, 6), dim), (blocks,), jnp.float32, smallest / len(pieces), high / len(pieces))
        factor_of = factor_of * jnp.repeat(jnp.exp(draws), dims[dim] // blocks).reshape((-1,) + (1,) * (len(dims) - 1 - dim))
    return factor_of


def bell_draw(own_key, dims, width, reach, split=(), held_as=jnp.bfloat16):
    values = jax.random.normal(own_key, dims, jnp.float32) * width
    if len(split) > 0:
        values = block_scale(own_key, dims, split, -0.22, 0.18) * values
    return jnp.clip(values, min=-reach, max=reach).astype(held_as)


def setup_inputs(seed: int = 0, part: int = 0) -> dict:
    key_of = jax.random.split(jax.random.key(seed), 11)
    part_keys = jax.random.split(jax.random.fold_in(key_of[10], part), 11)
    pressure_prev = bell_draw(part_keys[0], (LAYERS, NX, NY), 0.3, 2.5, ((1, 16),), jnp.float32)
    source = draw_source(jax.random.fold_in(jax.random.fold_in(key_of[10], part), 71), part)
    permeability = jnp.clip(jnp.exp(math.log(3.0) - 2.3025851 * jax.random.uniform(part_keys[2], (LAYERS, NX, NY), jnp.float32) ** block_scale(part_keys[2], (LAYERS, NX, NY), ((1, 16),), -0.2, 0.2)), 0.3, 3.0)
    region = place_ends(jax.random.randint(part_keys[3], (LAYERS, NX, NY), 0, REGIONS), jax.random.fold_in(part_keys[3], 1), 0, REGIONS - 1).astype(jnp.int32)
    region_factor = jnp.clip(jnp.exp(jax.random.uniform(part_keys[4], (REGIONS,), jnp.float32, math.log(0.3), math.log(3.0))), 0.3, 3.0)
    boundary = place_ends(jax.random.randint(part_keys[5], (LAYERS, NX, NY), 0, 3), jax.random.fold_in(part_keys[5], 1), 0, 2).astype(jnp.int32)
    flux_prev = bell_draw(part_keys[6], (3, LAYERS, NX, NY), 0.15, 2.0, ((2, 16),), jnp.float32)
    concentration = jnp.clip(0.2 + 1.8 * jax.random.uniform(part_keys[7], (SPECIES, LAYERS, NY, NX), jnp.float32) ** block_scale(part_keys[7], (SPECIES, LAYERS, NY, NX), ((2, 16),), -0.2, 0.2), 0.2, 2.0)
    porosity = jnp.clip(0.3 + 0.7 * jax.random.uniform(part_keys[8], (LAYERS, NY, NX), jnp.float32) ** block_scale(part_keys[8], (LAYERS, NY, NX), ((1, 16),), -0.2, 0.2), 0.3, 1.0)
    reaction = bell_draw(part_keys[9], (SPECIES, SPECIES), 0.5, 3.0, (), jnp.float32)
    return {"pressure_prev": pressure_prev, "source": source, "permeability": permeability, "region": region, "region_factor": region_factor, "boundary": boundary, "flux_prev": flux_prev, "concentration": concentration, "porosity": porosity, "reaction": reaction}


step_size = 0.5


def harmonic(left_val, right_val):
    return 2.0 * left_val * right_val / (left_val + right_val)


def pad_dim(tensor, along_dim, pad_before, pad_after):
    widths = [(0, 0)] * tensor.ndim
    widths[along_dim] = (pad_before, pad_after)
    return jnp.pad(tensor, widths)


def face_pair(conduct, along_dim):
    length = conduct.shape[along_dim]
    interior = harmonic(lax.slice_in_dim(conduct, 0, length - 1, axis=along_dim), lax.slice_in_dim(conduct, 1, length, axis=along_dim))
    padded = pad_dim(interior, along_dim, 1, 1)
    return lax.slice_in_dim(padded, 0, length, axis=along_dim), lax.slice_in_dim(padded, 1, length + 1, axis=along_dim)


def neighbours(field_in, along_dim):
    length = field_in.shape[along_dim]
    padded = pad_dim(field_in, along_dim, 1, 1)
    return lax.slice_in_dim(padded, 0, length, axis=along_dim), lax.slice_in_dim(padded, 2, length + 2, axis=along_dim)


def operate(field_in, diagonal, trans):
    below_x, above_x = neighbours(field_in, 1)
    below_y, above_y = neighbours(field_in, 2)
    below_z, above_z = neighbours(field_in, 0)
    return diagonal * field_in - (trans[0] * below_x + trans[1] * above_x + trans[2] * below_y + trans[3] * above_y + trans[4] * below_z + trans[5] * above_z)


def advect(species, face_flux, along_dim):
    length = species.shape[along_dim]
    padded = pad_dim(species, along_dim, 0, 1)
    below_cell = lax.slice_in_dim(padded, 0, length, axis=along_dim)
    above_cell = lax.slice_in_dim(padded, 1, length + 1, axis=along_dim)
    carried = face_flux * jnp.where(face_flux > 0, below_cell, above_cell)
    return carried - pad_dim(lax.slice_in_dim(carried, 0, length - 1, axis=along_dim), along_dim, 1, 0)


def reference(pressure_prev, source, permeability, region, region_factor, boundary, flux_prev, concentration, porosity, reaction):
    conduct = region_factor[region] * permeability
    lower_x, upper_x = face_pair(conduct, 1)
    lower_y, upper_y = face_pair(conduct, 2)
    lower_z, upper_z = face_pair(conduct, 0)
    leakage = jnp.where(boundary == 0, 0.05, jnp.where(boundary == 1, 1.0, 10.0)) * conduct
    diagonal = leakage + lower_x + upper_x + lower_y + upper_y + lower_z + upper_z
    trans = (lower_x, upper_x, lower_y, upper_y, lower_z, upper_z)
    pressure = pressure_prev
    residual = source - operate(pressure, diagonal, trans)
    precond = residual / diagonal
    direction = precond
    inner_now = jnp.sum(residual * precond)
    for sweep_index in range(ITERS):
        applied = operate(direction, diagonal, trans)
        step_len = inner_now / jnp.sum(direction * applied)
        pressure = pressure + step_len * direction
        residual = residual - step_len * applied
        precond = residual / diagonal
        inner_next = jnp.sum(residual * precond)
        direction = precond + (inner_next / inner_now) * direction
        inner_now = inner_next
    below_x, above_x = neighbours(pressure, 1)
    below_y, above_y = neighbours(pressure, 2)
    below_z, above_z = neighbours(pressure, 0)
    flux_new = jnp.stack([upper_x * (pressure - above_x), upper_y * (pressure - above_y), upper_z * (pressure - above_z)])
    turned = jnp.transpose(flux_prev, (0, 1, 3, 2))
    face_x = turned[0].at[:, :, -1].set(0.0)
    face_y = turned[1].at[:, -1, :].set(0.0)
    face_z = turned[2].at[-1].set(0.0)
    species = concentration
    for substep in range(SUBSTEPS):
        divergence = advect(species, face_y, 2) + advect(species, face_x, 3) + advect(species, face_z, 1)
        reaction_term = jnp.einsum("st,tzyx->szyx", reaction, species, precision=lax.Precision.HIGHEST)
        species = species - (step_size / porosity) * divergence + step_size * reaction_term
    return pressure, flux_new, species
```

```python
import jax
import jax.numpy as jnp
from jax import lax
from jax.experimental import pallas as pl
from jax.experimental.pallas import tpu as pltpu
from jax.sharding import PartitionSpec as P

step_size = 0.5
LANES = 128
WIDE = 3
MID = 2
EXT = 16
PAD = 24
BASE = 1
AXIS = "gx"


def odd_device():
    return lax.rem(lax.axis_index(AXIS), 2) == 1


def shifted(value, by):
    return pltpu.roll(value, by % value.shape[-1], value.ndim - 1)


def pack_halo(perm, region, rf, boundary, prev, source, conc, por, msg_a, msg_b, cond, leak):
    layers, rows, _ = perm.shape
    kinds = conc.shape[0]
    for z in range(layers):
        factor = jnp.zeros_like(perm[z])
        for r in range(rf.shape[0]):
            factor = jnp.where(region[z] == r, rf[r], factor)
        value = factor * perm[z]
        kind = boundary[z]
        cond[z] = value
        leak[z] = jnp.where(kind == 0, 0.05, jnp.where(kind == 1, 1.0, 10.0)) * value

    def fill(msg, low):
        wide = 0 if low else rows - WIDE
        mid = 0 if low else rows - MID
        one = 0 if low else rows - 1
        for z in range(layers):
            msg[z, 0:3] = cond[z, wide : wide + WIDE]
            msg[z, 3:6] = prev[z, wide : wide + WIDE]
            msg[z, 6:8] = source[z, mid : mid + MID]
            msg[layers + z, 0:2] = leak[z, mid : mid + MID]
            msg[layers + z, 2:3] = por[z, one : one + 1]
            for s in range(kinds):
                msg[2 * layers + z, 2 * s : 2 * s + 2] = conc[s, z, mid : mid + MID]

    odd = odd_device()

    @pl.when(odd)
    def _():
        fill(msg_a, True)
        fill(msg_b, False)

    @pl.when(jnp.logical_not(odd))
    def _():
        fill(msg_a, False)
        fill(msg_b, True)


def pack_flux(flux, out):
    layers, rows, width = flux.shape[1:]
    groups = LANES // rows
    spot = lax.rem(lax.broadcasted_iota(jnp.int32, (rows, width), 1), rows)
    block = lax.broadcasted_iota(jnp.int32, (rows, LANES), 1) // rows
    tall = [flux[c, z] for c in range(3) for z in range(layers)]
    for z in range(layers):
        along_x, along_y, along_z = flux[0, z], flux[1, z], flux[2, z]
        part = jnp.where(spot <= 1, shifted(along_y, 2), jnp.zeros_like(along_y))
        part = jnp.where(spot == 2, shifted(along_y, -(rows - 2)), part)
        part = jnp.where(spot == 3, shifted(along_x, 4), part)
        part = jnp.where(spot == 4, shifted(along_x, -(rows - 4)), part)
        part = jnp.where(spot == 5, shifted(along_z, 6), part)
        part = jnp.where(spot == 6, shifted(along_z, -(rows - 6)), part)
        tall.append(part)
    for m in range(width // LANES):
        v = [t[:, m * LANES : (m + 1) * LANES] for t in tall]
        d = 1
        while d < groups:
            keep = (block // d) % 2 == 0
            for g in range(groups):
                if g & d == 0:
                    a, b = v[g], v[g + d]
                    v[g] = jnp.where(keep, a, shifted(b, rows * d))
                    v[g + d] = jnp.where(keep, shifted(a, -rows * d), b)
            d *= 2
        for g in range(groups):
            out[m * groups + g] = v[g]


def harmonic(left_val, right_val):
    total = left_val + right_val
    return 2.0 * left_val * right_val / jnp.where(total > 0.0, total, 1.0)


def pressure_part(
    msg_a, msg_b, cond, leak, prev, source, packed, out, prev_e, u_e, z_e, tx_o, ty_o, tz_o, c_s, p_s, s_s, l_s, t_s
):
    layers, rows, width = cond.shape
    top = BASE + WIDE
    end = top + rows
    odd = odd_device()
    zeros = jnp.zeros((PAD, width), jnp.float32)
    for z in range(layers):
        first, second = msg_a[z], msg_b[z]
        low, high = jnp.where(odd, first, second), jnp.where(odd, second, first)
        first, second = msg_a[layers + z], msg_b[layers + z]
        low2, high2 = jnp.where(odd, first, second), jnp.where(odd, second, first)
        for buf, core, below, above, w in (
            (c_s, cond, low[0:3], high[0:3], WIDE),
            (p_s, prev, low[3:6], high[3:6], WIDE),
            (s_s, source, low[6:8], high[6:8], MID),
            (l_s, leak, low2[0:2], high2[0:2], MID),
        ):
            buf[z] = zeros
            buf[z, top - w : top] = below
            buf[z, top:end] = core[z]
            buf[z, end : end + w] = above
        t_s[z] = zeros
    here, up, down = pl.ds(BASE, EXT), pl.ds(BASE + 1, EXT), pl.ds(BASE - 1, EXT)
    lane = lax.broadcasted_iota(jnp.int32, (EXT, width), 1)
    upper_x, lower_x, upper_y, lower_y, upper_z, diagonal = [], [], [], [], [], []
    for z in range(layers):
        c = c_s[z, here]
        tx = harmonic(c, c_s[z, up])
        t_s[z, here] = tx
        ty = jnp.where(lane == width - 1, 0.0, harmonic(c, shifted(c, -1)))
        upper_x.append(tx)
        upper_y.append(ty)
        lower_y.append(shifted(ty, 1))
        upper_z.append(harmonic(c, c_s[z + 1, here]) if z + 1 < layers else None)
    for z in range(layers):
        lower_x.append(t_s[z, down])
        diag = l_s[z, here] + lower_x[z] + upper_x[z] + lower_y[z] + upper_y[z]
        if z > 0:
            diag = diag + upper_z[z - 1]
        if z + 1 < layers:
            diag = diag + upper_z[z]
        diagonal.append(diag)

    def around(buf):
        found = []
        for z in range(layers):
            v = buf[z, here]
            total = lower_x[z] * buf[z, down] + upper_x[z] * buf[z, up]
            total = total + lower_y[z] * shifted(v, 1) + upper_y[z] * shifted(v, -1)
            if z > 0:
                total = total + upper_z[z - 1] * buf[z - 1, here]
            if z + 1 < layers:
                total = total + upper_z[z] * buf[z + 1, here]
            found.append(total)
        return found

    inverse = [1.0 / jnp.where(d > 0.0, d, 1.0) for d in diagonal]
    from_prev = around(p_s)
    residual, u = [], []
    for z in range(layers):
        r = s_s[z, here] - (diagonal[z] * p_s[z, here] - from_prev[z])
        residual.append(r)
        u.append(r * inverse[z])
    for z in range(layers):
        s_s[z, here] = u[z]
    from_u = around(s_s)
    zed = [from_u[z] * inverse[z] for z in range(layers)]
    for z in range(layers):
        l_s[z] = zeros
        l_s[z, here] = zed[z]
    from_z = around(l_s)
    core_row = lax.broadcasted_iota(jnp.int32, (EXT, width), 0)
    inside = jnp.logical_and(core_row >= WIDE, core_row < WIDE + rows)

    def total_of(left, right):
        total = left[0] * right[0]
        for z in range(1, layers):
            total = total + left[z] * right[z]
        total = jnp.where(inside, total, 0.0)
        return jnp.sum(jnp.sum(total, axis=0, keepdims=True), axis=1, keepdims=True)

    sums = (total_of(residual, u), total_of(u, from_u), total_of(zed, from_u), total_of(zed, from_z))
    col = lax.broadcasted_iota(jnp.int32, (rows, LANES), 1)
    slots = col < 0
    value = jnp.zeros((rows, LANES), jnp.float32)
    for m, total in enumerate(sums):
        slot = col == (3 * layers + m) * rows + rows - 1
        slots = jnp.logical_or(slots, slot)
        value = jnp.where(slot, total, value)
    for k in range(packed.shape[0]):
        out[k] = jnp.where(slots, value, packed[k])
    for z in range(layers):
        prev_e[z] = p_s[z, here]
        u_e[z] = u[z]
        z_e[z] = zed[z]
        tx_o[z] = t_s[z, top:end]
        ty_o[z] = upper_y[z][WIDE : WIDE + rows]
        if z + 1 < layers:
            tz_o[z] = upper_z[z][WIDE : WIDE + rows]


def finish(
    arrived, msg_a, msg_b, conc, por, reaction, prev_e, u_e, z_e, tx, ty, tz,
    pressure, flux_new, species, turned, p_s, now_s, next_s, fx_s, fy_s, fz_s, por_s,
):
    kinds, layers, rows, width = conc.shape
    turned[...] = jnp.transpose(arrived[...].reshape(width, LANES))
    halo = 3 * layers * rows

    sums = [
        jnp.sum(turned[halo + rows * m + rows - 1 : halo + rows * (m + 1), :], axis=1, keepdims=True) * (1.0 / rows)
        for m in range(4)
    ]
    g, h, k, l = sums
    first = g / (g - h)
    rest = 1.0 - first
    gamma = rest * rest * g + 2.0 * first * rest * h + first * first * k
    weight = rest + gamma / g
    bend = weight * weight * (g - h) + 2.0 * weight * first * (h - k) + first * first * (k - l)
    second = gamma / bend
    of_u = first + second * weight
    of_z = second * first
    for z in range(layers):
        p_s[z] = prev_e[z] + of_u * u_e[z] + of_z * z_e[z]
    lane = lax.broadcasted_iota(jnp.int32, (rows, tx.shape[-1]), 1)
    for z in range(layers):
        p = p_s[z, WIDE : WIDE + rows]
        pressure[z] = p
        flux_new[0, z] = tx[z] * (p - p_s[z, WIDE + 1 : WIDE + 1 + rows])
        flux_new[1, z] = ty[z] * (p - shifted(p, -1))
        if z + 1 < layers:
            flux_new[2, z] = tz[z] * (p - p_s[z + 1, WIDE : WIDE + rows])
        else:
            flux_new[2, z] = jnp.zeros_like(p)

    odd = odd_device()
    index = lax.axis_index(AXIS)
    is_first, is_last = index == 0, index == lax.axis_size(AXIS) - 1
    top = BASE + MID
    end = top + rows
    zeros = jnp.zeros((PAD, width), jnp.float32)
    for z in range(layers):
        for buf, c in ((fx_s, 0), (fy_s, 1), (fz_s, 2)):
            buf[z] = zeros
            group = (c * layers + z) * rows
            buf[z, top:end] = turned[group : group + rows, :]
        extra = halo + rows * z
        fy_s[z, top - 2 : top] = turned[extra : extra + 2, :]
        fy_s[z, end : end + 1] = turned[extra + 2 : extra + 3, :]
        fx_s[z, top - 1 : top] = turned[extra + 3 : extra + 4, :]
        fx_s[z, end : end + 1] = turned[extra + 4 : extra + 5, :]
        fz_s[z, top - 1 : top] = turned[extra + 5 : extra + 6, :]
        fz_s[z, end : end + 1] = turned[extra + 6 : extra + 7, :]
        first_m, second_m = msg_a[layers + z, 2:3], msg_b[layers + z, 2:3]
        por_s[z] = zeros
        por_s[z, top - 1 : top] = jnp.where(odd, first_m, second_m)
        por_s[z, top:end] = por[z]
        por_s[z, end : end + 1] = jnp.where(odd, second_m, first_m)
        for s in range(kinds):
            first_m = msg_a[2 * layers + z, 2 * s : 2 * s + 2]
            second_m = msg_b[2 * layers + z, 2 * s : 2 * s + 2]
            now_s[s, z] = zeros
            now_s[s, z, top - MID : top] = jnp.where(odd, first_m, second_m)
            now_s[s, z, top:end] = conc[s, z]
            now_s[s, z, end : end + MID] = jnp.where(odd, second_m, first_m)
            next_s[s, z] = zeros

    @pl.when(is_first)
    def _():
        for z in range(layers):
            fy_s[z, top - 1 : top] = jnp.zeros((1, width), jnp.float32)

    @pl.when(is_last)
    def _():
        for z in range(layers):
            fy_s[z, end - 1 : end] = jnp.zeros((1, width), jnp.float32)

    def weights(start, count):
        lane = lax.broadcasted_iota(jnp.int32, (count, width), 1)
        here, down = pl.ds(start, count), pl.ds(start - 1, count)
        found = []
        carried_down = None
        for z in range(layers):
            pores = por_s[z, here]
            scale = step_size / jnp.where(pores > 0.0, pores, 1.0)
            fy, fy_low = fy_s[z, here], fy_s[z, down]
            fx = jnp.where(lane == width - 1, 0.0, fx_s[z, here])
            out_x, in_x = jnp.maximum(fx, 0.0), jnp.minimum(fx, 0.0)
            low_out, low_in = shifted(out_x, 1), shifted(in_x, 1)
            centre = jnp.maximum(fy, 0.0) - jnp.minimum(fy_low, 0.0) + out_x - low_in
            y_up, y_down = -scale * jnp.minimum(fy, 0.0), scale * jnp.maximum(fy_low, 0.0)
            x_up, x_down = -scale * in_x, scale * low_out
            z_up = z_down = None
            if z > 0:
                fz_low = carried_down
                centre = centre - jnp.minimum(fz_low, 0.0)
                z_down = scale * jnp.maximum(fz_low, 0.0)
            if z + 1 < layers:
                fz = fz_s[z, here]
                carried_down = fz
                centre = centre + jnp.maximum(fz, 0.0)
                z_up = -scale * jnp.minimum(fz, 0.0)
            found.append((1.0 - scale * centre, y_up, y_down, x_up, x_down, z_up, z_down))
        return found

    rate = [[step_size * reaction[s, t] for t in range(kinds)] for s in range(kinds)]

    def advance(buf, put, start, count, coefficients):
        here, up, down = pl.ds(start, count), pl.ds(start + 1, count), pl.ds(start - 1, count)
        for z in range(layers):
            centre, y_up, y_down, x_up, x_down, z_up, z_down = coefficients[z]
            cells = [buf[s, z, here] for s in range(kinds)]
            for s in range(kinds):
                v = cells[s]
                total = centre * v + y_up * buf[s, z, up] + y_down * buf[s, z, down]
                total = total + x_up * shifted(v, -1) + x_down * shifted(v, 1)
                if z > 0:
                    total = total + z_down * buf[s, z - 1, here]
                if z + 1 < layers:
                    total = total + z_up * buf[s, z + 1, here]
                for t in range(kinds):
                    total = total + rate[s][t] * cells[t]
                put(s, z, total)

    def put_next(s, z, value):
        next_s[s, z, BASE : BASE + EXT] = value

    def put_out(s, z, value):
        species[s, z] = value

    coefficients = weights(BASE, EXT)
    advance(now_s, put_next, BASE, EXT, coefficients)
    advance(next_s, put_out, top, rows, weights(top, rows))


def shards(
    pressure_prev, source, permeability, region, region_factor, boundary, flux_prev, concentration, porosity, reaction
):
    layers, rows, width = permeability.shape
    kinds = concentration.shape[0]
    peers = lax.axis_size(AXIS)
    assert rows * peers == width and concentration.shape[-1] == width
    assert rows == 8 and 4 * layers * rows == LANES and layers >= 4 and 2 * kinds <= rows
    f32 = jnp.float32
    vmem = pl.BlockSpec(memory_space=pltpu.VMEM)
    smem = pl.BlockSpec(memory_space=pltpu.SMEM)

    def arr(*shape):
        return jax.ShapeDtypeStruct(shape, f32)

    message = arr(3 * layers, rows, width)
    slab = arr(layers, rows, width)
    ext = arr(layers, EXT, width)
    chunks = arr(peers, rows, LANES)

    msg_a, msg_b, cond, leak = pl.pallas_call(
        pack_halo,
        name="pack_halo",
        out_shape=(message, message, slab, slab),
        in_specs=[vmem, vmem, smem, vmem, vmem, vmem, vmem, vmem],
        out_specs=(vmem,) * 4,
    )(permeability, region, region_factor, boundary, pressure_prev, source, concentration, porosity)
    partner = [(i, i + 1) for i in range(0, peers - 1, 2)]
    other = [(i, i + 1) for i in range(1, peers - 1, 2)]
    got_a = lax.ppermute(msg_a, AXIS, partner + [(j, i) for i, j in partner])
    got_b = lax.ppermute(msg_b, AXIS, other + [(j, i) for i, j in other])
    packed = pl.pallas_call(
        pack_flux, name="pack_flux", out_shape=chunks, in_specs=[vmem], out_specs=vmem
    )(flux_prev)
    pad = pltpu.VMEM((layers, PAD, width), f32)
    outgoing, prev_e, u_e, z_e, tx, ty, tz = pl.pallas_call(
        pressure_part,
        name="pressure_part",
        out_shape=(chunks, ext, ext, ext, slab, slab, arr(layers - 1, rows, width)),
        in_specs=[vmem] * 7,
        out_specs=(vmem,) * 7,
        scratch_shapes=[pad] * 5,
    )(got_a, got_b, cond, leak, pressure_prev, source, packed)
    arrived = lax.all_to_all(outgoing, AXIS, split_axis=0, concat_axis=0, tiled=True)
    cells = pltpu.VMEM((kinds, layers, PAD, width), f32)
    return pl.pallas_call(
        finish,
        name="finish",
        out_shape=(slab, arr(3, layers, rows, width), arr(kinds, layers, rows, width)),
        in_specs=[vmem] * 5 + [smem] + [vmem] * 6,
        out_specs=(vmem,) * 3,
        scratch_shapes=[pltpu.VMEM((LANES, width), f32), pltpu.VMEM((layers, EXT, width), f32), cells, cells]
        + [pad] * 4,
    )(arrived, got_a, got_b, concentration, porosity, reaction, prev_e, u_e, z_e, tx, ty, tz)


def solution(mesh):
    in_specs = (
        P("ens", "gx", None),
        P("ens", "gx", None),
        P("ens", "gx", None),
        P("ens", "gx", None),
        P("ens"),
        P("ens", "gx", None),
        P(None, "ens", "gx", None),
        P(None, "ens", "gx", None),
        P("ens", "gx", None),
        P("ens", None),
    )
    out_specs = (P("ens", "gx", None), P(None, "ens", "gx", None), P(None, "ens", "gx", None))
    return jax.shard_map(shards, mesh=mesh, in_specs=in_specs, out_specs=out_specs, check_vma=False)
```

```python
import jax
import jax.numpy as jnp
from jax import lax
from jax.experimental import pallas as pl
from jax.experimental.pallas import tpu as pltpu
from jax.sharding import PartitionSpec as P

step_size = 0.5
LANES = 128
WIDE = 3
MID = 2
EXT = 16
PAD = 24
BASE = 1
AXIS = "gx"


def odd_device():
    return lax.rem(lax.axis_index(AXIS), 2) == 1


def shifted(value, by):
    return pltpu.roll(value, by % value.shape[-1], value.ndim - 1)


def pack_halo(perm, region, rf, boundary, prev, source, conc, por, msg_a, msg_b, cond, leak):
    layers, rows, _ = perm.shape
    kinds = conc.shape[0]
    for z in range(layers):
        factor = jnp.zeros_like(perm[z])
        for r in range(rf.shape[0]):
            factor = jnp.where(region[z] == r, rf[r], factor)
        value = factor * perm[z]
        kind = boundary[z]
        cond[z] = value
        leak[z] = jnp.where(kind == 0, 0.05, jnp.where(kind == 1, 1.0, 10.0)) * value

    def fill(msg, low):
        wide = 0 if low else rows - WIDE
        mid = 0 if low else rows - MID
        one = 0 if low else rows - 1
        for z in range(layers):
            msg[z, 0:3] = cond[z, wide : wide + WIDE]
            msg[z, 3:6] = prev[z, wide : wide + WIDE]
            msg[z, 6:8] = source[z, mid : mid + MID]
            msg[layers + z, 0:2] = leak[z, mid : mid + MID]
            msg[layers + z, 2:3] = por[z, one : one + 1]
            for s in range(kinds):
                msg[2 * layers + z, 2 * s : 2 * s + 2] = conc[s, z, mid : mid + MID]

    odd = odd_device()

    @pl.when(odd)
    def _():
        fill(msg_a, True)
        fill(msg_b, False)

    @pl.when(jnp.logical_not(odd))
    def _():
        fill(msg_a, False)
        fill(msg_b, True)


def pack_flux(flux, out):
    layers, rows, width = flux.shape[1:]
    groups = LANES // rows
    spot = lax.rem(lax.broadcasted_iota(jnp.int32, (rows, width), 1), rows)
    block = lax.broadcasted_iota(jnp.int32, (rows, LANES), 1) // rows
    tall = [flux[c, z] for c in range(3) for z in range(layers)]
    for z in range(layers):
        along_x, along_y, along_z = flux[0, z], flux[1, z], flux[2, z]
        part = jnp.where(spot <= 1, shifted(along_y, 2), jnp.zeros_like(along_y))
        part = jnp.where(spot == 2, shifted(along_y, -(rows - 2)), part)
        part = jnp.where(spot == 3, shifted(along_x, 4), part)
        part = jnp.where(spot == 4, shifted(along_x, -(rows - 4)), part)
        part = jnp.where(spot == 5, shifted(along_z, 6), part)
        part = jnp.where(spot == 6, shifted(along_z, -(rows - 6)), part)
        tall.append(part)
    for m in range(width // LANES):
        v = [t[:, m * LANES : (m + 1) * LANES] for t in tall]
        d = 1
        while d < groups:
            keep = (block // d) % 2 == 0
            for g in range(groups):
                if g & d == 0:
                    a, b = v[g], v[g + d]
                    v[g] = jnp.where(keep, a, shifted(b, rows * d))
                    v[g + d] = jnp.where(keep, shifted(a, -rows * d), b)
            d *= 2
        for g in range(groups):
            out[m * groups + g] = v[g]


def harmonic(left_val, right_val):
    total = left_val + right_val
    return 2.0 * left_val * right_val / jnp.where(total > 0.0, total, 1.0)


def pressure_part(
    msg_a, msg_b, cond, leak, prev, source, packed, out, prev_e, u_e, z_e, tx_o, ty_o, tz_o, c_s, p_s, s_s, l_s, t_s
):
    layers, rows, width = cond.shape
    top = BASE + WIDE
    end = top + rows
    odd = odd_device()
    zeros = jnp.zeros((PAD, width), jnp.float32)
    for z in range(layers):
        first, second = msg_a[z], msg_b[z]
        low, high = jnp.where(odd, first, second), jnp.where(odd, second, first)
        first, second = msg_a[layers + z], msg_b[layers + z]
        low2, high2 = jnp.where(odd, first, second), jnp.where(odd, second, first)
        for buf, core, below, above, w in (
            (c_s, cond, low[0:3], high[0:3], WIDE),
            (p_s, prev, low[3:6], high[3:6], WIDE),
            (s_s, source, low[6:8], high[6:8], MID),
            (l_s, leak, low2[0:2], high2[0:2], MID),
        ):
            buf[z] = zeros
            buf[z, top - w : top] = below
            buf[z, top:end] = core[z]
            buf[z, end : end + w] = above
        t_s[z] = zeros
    here, up, down = pl.ds(BASE, EXT), pl.ds(BASE + 1, EXT), pl.ds(BASE - 1, EXT)
    lane = lax.broadcasted_iota(jnp.int32, (EXT, width), 1)
    upper_x, lower_x, upper_y, lower_y, upper_z, diagonal = [], [], [], [], [], []
    for z in range(layers):
        c = c_s[z, here]
        tx = harmonic(c, c_s[z, up])
        t_s[z, here] = tx
        ty = jnp.where(lane == width - 1, 0.0, harmonic(c, shifted(c, -1)))
        upper_x.append(tx)
        upper_y.append(ty)
        lower_y.append(shifted(ty, 1))
        upper_z.append(harmonic(c, c_s[z + 1, here]) if z + 1 < layers else None)
    for z in range(layers):
        lower_x.append(t_s[z, down])
        diag = l_s[z, here] + lower_x[z] + upper_x[z] + lower_y[z] + upper_y[z]
        if z > 0:
            diag = diag + upper_z[z - 1]
        if z + 1 < layers:
            diag = diag + upper_z[z]
        diagonal.append(diag)

    def around(buf):
        found = []
        for z in range(layers):
            v = buf[z, here]
            total = lower_x[z] * buf[z, down] + upper_x[z] * buf[z, up]
            total = total + lower_y[z] * shifted(v, 1) + upper_y[z] * shifted(v, -1)
            if z > 0:
                total = total + upper_z[z - 1] * buf[z - 1, here]
            if z + 1 < layers:
                total = total + upper_z[z] * buf[z + 1, here]
            found.append(total)
        return found

    inverse = [1.0 / jnp.where(d > 0.0, d, 1.0) for d in diagonal]
    from_prev = around(p_s)
    residual, u = [], []
    for z in range(layers):
        r = s_s[z, here] - (diagonal[z] * p_s[z, here] - from_prev[z])
        residual.append(r)
        u.append(r * inverse[z])
    for z in range(layers):
        s_s[z, here] = u[z]
    from_u = around(s_s)
    zed = [from_u[z] * inverse[z] for z in range(layers)]
    for z in range(layers):
        l_s[z] = zeros
        l_s[z, here] = zed[z]
    from_z = around(l_s)
    core_row = lax.broadcasted_iota(jnp.int32, (EXT, width), 0)
    inside = jnp.logical_and(core_row >= WIDE, core_row < WIDE + rows)

    def total_of(left, right):
        total = left[0] * right[0]
        for z in range(1, layers):
            total = total + left[z] * right[z]
        total = jnp.where(inside, total, 0.0)
        return jnp.sum(jnp.sum(total, axis=0, keepdims=True), axis=1, keepdims=True)

    sums = (total_of(residual, u), total_of(u, from_u), total_of(zed, from_u), total_of(zed, from_z))
    col = lax.broadcasted_iota(jnp.int32, (rows, LANES), 1)
    slots = col < 0
    value = jnp.zeros((rows, LANES), jnp.float32)
    for m, total in enumerate(sums):
        slot = col == (3 * layers + m) * rows + rows - 1
        slots = jnp.logical_or(slots, slot)
        value = jnp.where(slot, total, value)
    for k in range(packed.shape[0]):
        out[k] = jnp.where(slots, value, packed[k])
    for z in range(layers):
        prev_e[z] = p_s[z, here]
        u_e[z] = u[z]
        z_e[z] = zed[z]
        tx_o[z] = t_s[z, top:end]
        ty_o[z] = upper_y[z][WIDE : WIDE + rows]
        if z + 1 < layers:
            tz_o[z] = upper_z[z][WIDE : WIDE + rows]


def finish(
    arrived, msg_a, msg_b, conc, por, reaction, prev_e, u_e, z_e, tx, ty, tz,
    pressure, flux_new, species, turned, p_s, now_s, next_s, fx_s, fy_s, fz_s, por_s,
):
    kinds, layers, rows, width = conc.shape
    turned[...] = jnp.transpose(arrived[...].reshape(width, LANES))
    halo = 3 * layers * rows

    sums = [
        jnp.sum(turned[halo + rows * m + rows - 1 : halo + rows * (m + 1), :], axis=1, keepdims=True) * (1.0 / rows)
        for m in range(4)
    ]
    g, h, k, l = sums
    first = g / (g - h)
    rest = 1.0 - first
    gamma = rest * rest * g + 2.0 * first * rest * h + first * first * k
    weight = rest + gamma / g
    bend = weight * weight * (g - h) + 2.0 * weight * first * (h - k) + first * first * (k - l)
    second = gamma / bend
    of_u = first + second * weight
    of_z = second * first
    for z in range(layers):
        p_s[z] = prev_e[z] + of_u * u_e[z] + of_z * z_e[z]
    lane = lax.broadcasted_iota(jnp.int32, (rows, tx.shape[-1]), 1)
    for z in range(layers):
        p = p_s[z, WIDE : WIDE + rows]
        pressure[z] = p
        flux_new[0, z] = tx[z] * (p - p_s[z, WIDE + 1 : WIDE + 1 + rows])
        flux_new[1, z] = ty[z] * (p - shifted(p, -1))
        if z + 1 < layers:
            flux_new[2, z] = tz[z] * (p - p_s[z + 1, WIDE : WIDE + rows])
        else:
            flux_new[2, z] = jnp.zeros_like(p)

    odd = odd_device()
    index = lax.axis_index(AXIS)
    is_first, is_last = index == 0, index == lax.axis_size(AXIS) - 1
    top = BASE + MID
    end = top + rows
    zeros = jnp.zeros((PAD, width), jnp.float32)
    for z in range(layers):
        for buf, c in ((fx_s, 0), (fy_s, 1), (fz_s, 2)):
            buf[z] = zeros
            group = (c * layers + z) * rows
            buf[z, top:end] = turned[group : group + rows, :]
        extra = halo + rows * z
        fy_s[z, top - 2 : top] = turned[extra : extra + 2, :]
        fy_s[z, end : end + 1] = turned[extra + 2 : extra + 3, :]
        fx_s[z, top - 1 : top] = turned[extra + 3 : extra + 4, :]
        fx_s[z, end : end + 1] = turned[extra + 4 : extra + 5, :]
        fz_s[z, top - 1 : top] = turned[extra + 5 : extra + 6, :]
        fz_s[z, end : end + 1] = turned[extra + 6 : extra + 7, :]
        first_m, second_m = msg_a[layers + z, 2:3], msg_b[layers + z, 2:3]
        por_s[z] = zeros
        por_s[z, top - 1 : top] = jnp.where(odd, first_m, second_m)
        por_s[z, top:end] = por[z]
        por_s[z, end : end + 1] = jnp.where(odd, second_m, first_m)
        for s in range(kinds):
            first_m = msg_a[2 * layers + z, 2 * s : 2 * s + 2]
            second_m = msg_b[2 * layers + z, 2 * s : 2 * s + 2]
            now_s[s, z] = zeros
            now_s[s, z, top - MID : top] = jnp.where(odd, first_m, second_m)
            now_s[s, z, top:end] = conc[s, z]
            now_s[s, z, end : end + MID] = jnp.where(odd, second_m, first_m)
            next_s[s, z] = zeros

    @pl.when(is_first)
    def _():
        for z in range(layers):
            fy_s[z, top - 1 : top] = jnp.zeros((1, width), jnp.float32)

    @pl.when(is_last)
    def _():
        for z in range(layers):
            fy_s[z, end - 1 : end] = jnp.zeros((1, width), jnp.float32)

    def weights(start, count):
        lane = lax.broadcasted_iota(jnp.int32, (count, width), 1)
        here, down = pl.ds(start, count), pl.ds(start - 1, count)
        found = []
        carried_down = None
        for z in range(layers):
            pores = por_s[z, here]
            scale = step_size / jnp.where(pores > 0.0, pores, 1.0)
            fy, fy_low = fy_s[z, here], fy_s[z, down]
            fx = jnp.where(lane == width - 1, 0.0, fx_s[z, here])
            out_x, in_x = jnp.maximum(fx, 0.0), jnp.minimum(fx, 0.0)
            low_out, low_in = shifted(out_x, 1), shifted(in_x, 1)
            centre = jnp.maximum(fy, 0.0) - jnp.minimum(fy_low, 0.0) + out_x - low_in
            y_up, y_down = -scale * jnp.minimum(fy, 0.0), scale * jnp.maximum(fy_low, 0.0)
            x_up, x_down = -scale * in_x, scale * low_out
            z_up = z_down = None
            if z > 0:
                fz_low = carried_down
                centre = centre - jnp.minimum(fz_low, 0.0)
                z_down = scale * jnp.maximum(fz_low, 0.0)
            if z + 1 < layers:
                fz = fz_s[z, here]
                carried_down = fz
                centre = centre + jnp.maximum(fz, 0.0)
                z_up = -scale * jnp.minimum(fz, 0.0)
            found.append((1.0 - scale * centre, y_up, y_down, x_up, x_down, z_up, z_down))
        return found

    rate = [[step_size * reaction[s, t] for t in range(kinds)] for s in range(kinds)]

    def advance(buf, put, start, count, coefficients):
        here, up, down = pl.ds(start, count), pl.ds(start + 1, count), pl.ds(start - 1, count)
        for z in range(layers):
            centre, y_up, y_down, x_up, x_down, z_up, z_down = coefficients[z]
            cells = [buf[s, z, here] for s in range(kinds)]
            for s in range(kinds):
                v = cells[s]
                total = centre * v + y_up * buf[s, z, up] + y_down * buf[s, z, down]
                total = total + x_up * shifted(v, -1) + x_down * shifted(v, 1)
                if z > 0:
                    total = total + z_down * buf[s, z - 1, here]
                if z + 1 < layers:
                    total = total + z_up * buf[s, z + 1, here]
                for t in range(kinds):
                    total = total + rate[s][t] * cells[t]
                put(s, z, total)

    def put_next(s, z, value):
        next_s[s, z, BASE : BASE + EXT] = value

    def put_out(s, z, value):
        species[s, z] = value

    coefficients = weights(BASE, EXT)
    advance(now_s, put_next, BASE, EXT, coefficients)
    advance(next_s, put_out, top, rows, weights(top, rows))


def shards(
    pressure_prev, source, permeability, region, region_factor, boundary, flux_prev, concentration, porosity, reaction
):
    layers, rows, width = permeability.shape
    kinds = concentration.shape[0]
    peers = lax.axis_size(AXIS)
    assert rows * peers == width and concentration.shape[-1] == width
    assert rows == 8 and 4 * layers * rows == LANES and layers >= 4 and 2 * kinds <= rows
    f32 = jnp.float32
    vmem = pl.BlockSpec(memory_space=pltpu.VMEM)
    smem = pl.BlockSpec(memory_space=pltpu.SMEM)

    def arr(*shape):
        return jax.ShapeDtypeStruct(shape, f32)

    def near(*shape):
        return pltpu.VMEM(shape, f32)

    def keep(*arrays):
        return [pltpu.with_memory_space_constraint(a, pltpu.VMEM) for a in arrays]

    message = near(3 * layers, rows, width)
    slab = near(layers, rows, width)
    ext = near(layers, EXT, width)
    chunks = near(peers, rows, LANES)

    msg_a, msg_b, cond, leak = pl.pallas_call(
        pack_halo,
        name="pack_halo",
        out_shape=(message, message, slab, slab),
        in_specs=[vmem, vmem, smem, vmem, vmem, vmem, vmem, vmem],
        out_specs=(vmem,) * 4,
    )(permeability, region, region_factor, boundary, pressure_prev, source, concentration, porosity)
    partner = [(i, i + 1) for i in range(0, peers - 1, 2)]
    other = [(i, i + 1) for i in range(1, peers - 1, 2)]
    got_a = lax.ppermute(msg_a, AXIS, partner + [(j, i) for i, j in partner])
    got_b = lax.ppermute(msg_b, AXIS, other + [(j, i) for i, j in other])
    packed = pl.pallas_call(
        pack_flux, name="pack_flux", out_shape=chunks, in_specs=[vmem], out_specs=vmem
    )(flux_prev)
    pad = pltpu.VMEM((layers, PAD, width), f32)
    outgoing, prev_e, u_e, z_e, tx, ty, tz = pl.pallas_call(
        pressure_part,
        name="pressure_part",
        out_shape=(chunks, ext, ext, ext, slab, slab, near(layers - 1, rows, width)),
        in_specs=[vmem] * 7,
        out_specs=(vmem,) * 7,
        scratch_shapes=[pad] * 5,
    )(*keep(got_a, got_b, cond, leak, pressure_prev, source, packed))
    arrived = lax.all_to_all(outgoing, AXIS, split_axis=0, concat_axis=0, tiled=True)
    cells = pltpu.VMEM((kinds, layers, PAD, width), f32)
    return pl.pallas_call(
        finish,
        name="finish",
        out_shape=(arr(layers, rows, width), arr(3, layers, rows, width), arr(kinds, layers, rows, width)),
        in_specs=[vmem] * 5 + [smem] + [vmem] * 6,
        out_specs=(vmem,) * 3,
        scratch_shapes=[pltpu.VMEM((LANES, width), f32), pltpu.VMEM((layers, EXT, width), f32), cells, cells]
        + [pad] * 4,
    )(*keep(arrived, got_a, got_b, concentration, porosity), reaction, *keep(prev_e, u_e, z_e, tx, ty, tz))


def solution(mesh):
    in_specs = (
        P("ens", "gx", None),
        P("ens", "gx", None),
        P("ens", "gx", None),
        P("ens", "gx", None),
        P("ens"),
        P("ens", "gx", None),
        P(None, "ens", "gx", None),
        P(None, "ens", "gx", None),
        P("ens", "gx", None),
        P("ens", None),
    )
    out_specs = (P("ens", "gx", None), P(None, "ens", "gx", None), P(None, "ens", "gx", None))
    return jax.shard_map(shards, mesh=mesh, in_specs=in_specs, out_specs=out_specs, check_vma=False)
```

```python
import jax
import jax.numpy as jnp
from jax import lax
from jax.experimental import pallas as pl
from jax.experimental.pallas import tpu as pltpu
from jax.sharding import PartitionSpec as P

step_size = 0.5
LANES = 128
WIDE = 3
MID = 2
EXT = 16
PAD = 24
BASE = 1
AXIS = "gx"
PARTS = "ens"


def odd_device():
    return lax.rem(lax.axis_index(AXIS), 2) == 1


def at_ends():
    index = lax.axis_index(AXIS)
    return index == 0, index == lax.axis_size(AXIS) - 1


def shifted(value, by):
    return pltpu.roll(value, by % value.shape[-1], value.ndim - 1)


def pack_halo(perm, region, rf, boundary, prev, source, conc, por, msg_a, msg_b, cond, leak):
    layers, rows, _ = perm.shape
    kinds = conc.shape[0]
    for z in range(layers):
        factor = jnp.zeros_like(perm[z])
        for r in range(rf.shape[0]):
            factor = jnp.where(region[z] == r, rf[r], factor)
        value = factor * perm[z]
        kind = boundary[z]
        cond[z] = value
        leak[z] = jnp.where(kind == 0, 0.05, jnp.where(kind == 1, 1.0, 10.0)) * value

    def fill(msg, low):
        wide = 0 if low else rows - WIDE
        mid = 0 if low else rows - MID
        one = 0 if low else rows - 1
        for z in range(layers):
            msg[z, 0:3] = cond[z, wide : wide + WIDE]
            msg[z, 3:6] = prev[z, wide : wide + WIDE]
            msg[z, 6:8] = source[z, mid : mid + MID]
            msg[layers + z, 0:2] = leak[z, mid : mid + MID]
            msg[layers + z, 2:3] = por[z, one : one + 1]
            for s in range(kinds):
                msg[2 * layers + z, 2 * s : 2 * s + 2] = conc[s, z, mid : mid + MID]

    odd = odd_device()

    @pl.when(odd)
    def _():
        fill(msg_a, True)
        fill(msg_b, False)

    @pl.when(jnp.logical_not(odd))
    def _():
        fill(msg_a, False)
        fill(msg_b, True)


def pack_flux(flux, out):
    layers, rows, width = flux.shape[1:]
    groups = LANES // rows
    spot = lax.rem(lax.broadcasted_iota(jnp.int32, (rows, width), 1), rows)
    block = lax.broadcasted_iota(jnp.int32, (rows, LANES), 1) // rows
    tall = [flux[c, z] for c in range(3) for z in range(layers)]
    for z in range(layers):
        along_x, along_y, along_z = flux[0, z], flux[1, z], flux[2, z]
        part = jnp.where(spot <= 1, shifted(along_y, 2), jnp.zeros_like(along_y))
        part = jnp.where(spot == 2, shifted(along_y, -(rows - 2)), part)
        part = jnp.where(spot == 3, shifted(along_x, 4), part)
        part = jnp.where(spot == 4, shifted(along_x, -(rows - 4)), part)
        part = jnp.where(spot == 5, shifted(along_z, 6), part)
        part = jnp.where(spot == 6, shifted(along_z, -(rows - 6)), part)
        tall.append(part)
    for m in range(width // LANES):
        v = [t[:, m * LANES : (m + 1) * LANES] for t in tall]
        d = 1
        while d < groups:
            keep = (block // d) % 2 == 0
            for g in range(groups):
                if g & d == 0:
                    a, b = v[g], v[g + d]
                    v[g] = jnp.where(keep, a, shifted(b, rows * d))
                    v[g + d] = jnp.where(keep, shifted(a, -rows * d), b)
            d *= 2
        for g in range(groups):
            out[m * groups + g] = v[g]


def harmonic(left_val, right_val):
    total = left_val + right_val
    return 2.0 * left_val * right_val / jnp.where(total > 0.0, total, 1.0)


def pressure_part(
    msg_a, msg_b, cond, leak, prev, source, packed, out, prev_e, u_e, z_e, tx_o, ty_o, tz_o, c_s, p_s, s_s, l_s, t_s
):
    layers, rows, width = cond.shape
    top = BASE + WIDE
    end = top + rows
    odd = odd_device()
    zeros = jnp.zeros((PAD, width), jnp.float32)
    for z in range(layers):
        first, second = msg_a[z], msg_b[z]
        low, high = jnp.where(odd, first, second), jnp.where(odd, second, first)
        first, second = msg_a[layers + z], msg_b[layers + z]
        low2, high2 = jnp.where(odd, first, second), jnp.where(odd, second, first)
        for buf, core, below, above, w in (
            (c_s, cond, low[0:3], high[0:3], WIDE),
            (p_s, prev, low[3:6], high[3:6], WIDE),
            (s_s, source, low[6:8], high[6:8], MID),
            (l_s, leak, low2[0:2], high2[0:2], MID),
        ):
            buf[z] = zeros
            buf[z, top - w : top] = below
            buf[z, top:end] = core[z]
            buf[z, end : end + w] = above
        t_s[z] = zeros

    is_first, is_last = at_ends()

    @pl.when(is_first)
    def _():
        for z in range(layers):
            for buf in (c_s, p_s, s_s, l_s):
                buf[z, BASE:top] = zeros[BASE:top]

    @pl.when(is_last)
    def _():
        for z in range(layers):
            for buf in (c_s, p_s, s_s, l_s):
                buf[z, end : end + WIDE] = zeros[:WIDE]

    here, up, down = pl.ds(BASE, EXT), pl.ds(BASE + 1, EXT), pl.ds(BASE - 1, EXT)
    lane = lax.broadcasted_iota(jnp.int32, (EXT, width), 1)
    upper_x, lower_x, upper_y, lower_y, upper_z, diagonal = [], [], [], [], [], []
    for z in range(layers):
        c = c_s[z, here]
        tx = harmonic(c, c_s[z, up])
        t_s[z, here] = tx
        ty = jnp.where(lane == width - 1, 0.0, harmonic(c, shifted(c, -1)))
        upper_x.append(tx)
        upper_y.append(ty)
        lower_y.append(shifted(ty, 1))
        upper_z.append(harmonic(c, c_s[z + 1, here]) if z + 1 < layers else None)
    for z in range(layers):
        lower_x.append(t_s[z, down])
        diag = l_s[z, here] + lower_x[z] + upper_x[z] + lower_y[z] + upper_y[z]
        if z > 0:
            diag = diag + upper_z[z - 1]
        if z + 1 < layers:
            diag = diag + upper_z[z]
        diagonal.append(diag)

    def around(buf):
        found = []
        for z in range(layers):
            v = buf[z, here]
            total = lower_x[z] * buf[z, down] + upper_x[z] * buf[z, up]
            total = total + lower_y[z] * shifted(v, 1) + upper_y[z] * shifted(v, -1)
            if z > 0:
                total = total + upper_z[z - 1] * buf[z - 1, here]
            if z + 1 < layers:
                total = total + upper_z[z] * buf[z + 1, here]
            found.append(total)
        return found

    inverse = [1.0 / jnp.where(d > 0.0, d, 1.0) for d in diagonal]
    from_prev = around(p_s)
    residual, u = [], []
    for z in range(layers):
        r = s_s[z, here] - (diagonal[z] * p_s[z, here] - from_prev[z])
        residual.append(r)
        u.append(r * inverse[z])
    for z in range(layers):
        s_s[z, here] = u[z]
    from_u = around(s_s)
    zed = [from_u[z] * inverse[z] for z in range(layers)]
    for z in range(layers):
        l_s[z] = zeros
        l_s[z, here] = zed[z]
    from_z = around(l_s)
    core_row = lax.broadcasted_iota(jnp.int32, (EXT, width), 0)
    inside = jnp.logical_and(core_row >= WIDE, core_row < WIDE + rows)

    def total_of(left, right):
        total = left[0] * right[0]
        for z in range(1, layers):
            total = total + left[z] * right[z]
        total = jnp.where(inside, total, 0.0)
        return jnp.sum(jnp.sum(total, axis=0, keepdims=True), axis=1, keepdims=True)

    sums = (total_of(residual, u), total_of(u, from_u), total_of(zed, from_u), total_of(zed, from_z))
    col = lax.broadcasted_iota(jnp.int32, (rows, LANES), 1)
    slots = col < 0
    value = jnp.zeros((rows, LANES), jnp.float32)
    for m, total in enumerate(sums):
        slot = col == (3 * layers + m) * rows + rows - 1
        slots = jnp.logical_or(slots, slot)
        value = jnp.where(slot, total, value)
    for k in range(packed.shape[0]):
        out[k] = jnp.where(slots, value, packed[k])
    for z in range(layers):
        prev_e[z] = p_s[z, here]
        u_e[z] = u[z]
        z_e[z] = zed[z]
        tx_o[z] = t_s[z, top:end]
        ty_o[z] = upper_y[z][WIDE : WIDE + rows]
        if z + 1 < layers:
            tz_o[z] = upper_z[z][WIDE : WIDE + rows]


def finish(
    arrived, msg_a, msg_b, conc, por, reaction, prev_e, u_e, z_e, tx, ty, tz,
    pressure, flux_new, species, turned, p_s, now_s, next_s, fx_s, fy_s, fz_s, por_s,
):
    kinds, layers, rows, width = conc.shape
    turned[...] = jnp.transpose(arrived[...].reshape(width, LANES))
    halo = 3 * layers * rows

    sums = [
        jnp.sum(turned[halo + rows * m + rows - 1 : halo + rows * (m + 1), :], axis=1, keepdims=True) * (1.0 / rows)
        for m in range(4)
    ]
    g, h, k, l = sums
    first = g / (g - h)
    rest = 1.0 - first
    gamma = rest * rest * g + 2.0 * first * rest * h + first * first * k
    weight = rest + gamma / g
    bend = weight * weight * (g - h) + 2.0 * weight * first * (h - k) + first * first * (k - l)
    second = gamma / bend
    of_u = first + second * weight
    of_z = second * first
    for z in range(layers):
        p_s[z] = prev_e[z] + of_u * u_e[z] + of_z * z_e[z]
    lane = lax.broadcasted_iota(jnp.int32, (rows, tx.shape[-1]), 1)
    for z in range(layers):
        p = p_s[z, WIDE : WIDE + rows]
        pressure[z] = p
        flux_new[0, z] = tx[z] * (p - p_s[z, WIDE + 1 : WIDE + 1 + rows])
        flux_new[1, z] = ty[z] * (p - shifted(p, -1))
        if z + 1 < layers:
            flux_new[2, z] = tz[z] * (p - p_s[z + 1, WIDE : WIDE + rows])
        else:
            flux_new[2, z] = jnp.zeros_like(p)

    odd = odd_device()
    is_first, is_last = at_ends()
    top = BASE + MID
    end = top + rows
    zeros = jnp.zeros((PAD, width), jnp.float32)
    for z in range(layers):
        for buf, c in ((fx_s, 0), (fy_s, 1), (fz_s, 2)):
            buf[z] = zeros
            group = (c * layers + z) * rows
            buf[z, top:end] = turned[group : group + rows, :]
        extra = halo + rows * z
        fy_s[z, top - 2 : top] = turned[extra : extra + 2, :]
        fy_s[z, end : end + 1] = turned[extra + 2 : extra + 3, :]
        fx_s[z, top - 1 : top] = turned[extra + 3 : extra + 4, :]
        fx_s[z, end : end + 1] = turned[extra + 4 : extra + 5, :]
        fz_s[z, top - 1 : top] = turned[extra + 5 : extra + 6, :]
        fz_s[z, end : end + 1] = turned[extra + 6 : extra + 7, :]
        first_m, second_m = msg_a[layers + z, 2:3], msg_b[layers + z, 2:3]
        por_s[z] = zeros
        por_s[z, top - 1 : top] = jnp.where(odd, first_m, second_m)
        por_s[z, top:end] = por[z]
        por_s[z, end : end + 1] = jnp.where(odd, second_m, first_m)
        for s in range(kinds):
            first_m = msg_a[2 * layers + z, 2 * s : 2 * s + 2]
            second_m = msg_b[2 * layers + z, 2 * s : 2 * s + 2]
            now_s[s, z] = zeros
            now_s[s, z, top - MID : top] = jnp.where(odd, first_m, second_m)
            now_s[s, z, top:end] = conc[s, z]
            now_s[s, z, end : end + MID] = jnp.where(odd, second_m, first_m)
            next_s[s, z] = zeros

    @pl.when(is_first)
    def _():
        for z in range(layers):
            fy_s[z, top - 1 : top] = jnp.zeros((1, width), jnp.float32)

    @pl.when(is_last)
    def _():
        for z in range(layers):
            fy_s[z, end - 1 : end] = jnp.zeros((1, width), jnp.float32)

    def weights(start, count):
        lane = lax.broadcasted_iota(jnp.int32, (count, width), 1)
        here, down = pl.ds(start, count), pl.ds(start - 1, count)
        found = []
        carried_down = None
        for z in range(layers):
            pores = por_s[z, here]
            scale = step_size / jnp.where(pores > 0.0, pores, 1.0)
            fy, fy_low = fy_s[z, here], fy_s[z, down]
            fx = jnp.where(lane == width - 1, 0.0, fx_s[z, here])
            out_x, in_x = jnp.maximum(fx, 0.0), jnp.minimum(fx, 0.0)
            low_out, low_in = shifted(out_x, 1), shifted(in_x, 1)
            centre = jnp.maximum(fy, 0.0) - jnp.minimum(fy_low, 0.0) + out_x - low_in
            y_up, y_down = -scale * jnp.minimum(fy, 0.0), scale * jnp.maximum(fy_low, 0.0)
            x_up, x_down = -scale * in_x, scale * low_out
            z_up = z_down = None
            if z > 0:
                fz_low = carried_down
                centre = centre - jnp.minimum(fz_low, 0.0)
                z_down = scale * jnp.maximum(fz_low, 0.0)
            if z + 1 < layers:
                fz = fz_s[z, here]
                carried_down = fz
                centre = centre + jnp.maximum(fz, 0.0)
                z_up = -scale * jnp.minimum(fz, 0.0)
            found.append((1.0 - scale * centre, y_up, y_down, x_up, x_down, z_up, z_down))
        return found

    rate = [[step_size * reaction[s, t] for t in range(kinds)] for s in range(kinds)]

    def advance(buf, put, start, count, coefficients):
        here, up, down = pl.ds(start, count), pl.ds(start + 1, count), pl.ds(start - 1, count)
        for z in range(layers):
            centre, y_up, y_down, x_up, x_down, z_up, z_down = coefficients[z]
            cells = [buf[s, z, here] for s in range(kinds)]
            for s in range(kinds):
                v = cells[s]
                total = centre * v + y_up * buf[s, z, up] + y_down * buf[s, z, down]
                total = total + x_up * shifted(v, -1) + x_down * shifted(v, 1)
                if z > 0:
                    total = total + z_down * buf[s, z - 1, here]
                if z + 1 < layers:
                    total = total + z_up * buf[s, z + 1, here]
                for t in range(kinds):
                    total = total + rate[s][t] * cells[t]
                put(s, z, total)

    def put_next(s, z, value):
        next_s[s, z, BASE : BASE + EXT] = value

    def put_out(s, z, value):
        species[s, z] = value

    coefficients = weights(BASE, EXT)
    advance(now_s, put_next, BASE, EXT, coefficients)
    advance(next_s, put_out, top, rows, weights(top, rows))


def exchange(msg_a, msg_b):
    peers, parts = lax.axis_size(AXIS), lax.axis_size(PARTS)
    assert peers % 2 == 0
    partner = [(i, i + 1) for i in range(0, peers, 2)]
    other = [(i, i + 1) for i in range(1, peers - 1, 2)]
    pairs = [(e * peers + i, e * peers + j) for e in range(parts) for i, j in other]
    pairs += [(e * peers + i, (e + 1) * peers + i) for e in range(0, parts - 1, 2) for i in (0, peers - 1)]
    got_a = lax.ppermute(msg_a, AXIS, partner + [(j, i) for i, j in partner])
    got_b = lax.ppermute(msg_b, (PARTS, AXIS), pairs + [(j, i) for i, j in pairs])
    return got_a, got_b


def shards(
    pressure_prev, source, permeability, region, region_factor, boundary, flux_prev, concentration, porosity, reaction
):
    layers, rows, width = permeability.shape
    kinds = concentration.shape[0]
    peers = lax.axis_size(AXIS)
    assert rows * peers == width and concentration.shape[-1] == width
    assert rows == 8 and 4 * layers * rows == LANES and layers >= 4 and 2 * kinds <= rows
    f32 = jnp.float32
    vmem = pl.BlockSpec(memory_space=pltpu.VMEM)
    smem = pl.BlockSpec(memory_space=pltpu.SMEM)

    def arr(*shape):
        return jax.ShapeDtypeStruct(shape, f32)

    def near(*shape):
        return pltpu.VMEM(shape, f32)

    def keep(*arrays):
        return [pltpu.with_memory_space_constraint(a, pltpu.VMEM) for a in arrays]

    message = near(3 * layers, rows, width)
    slab = near(layers, rows, width)
    ext = near(layers, EXT, width)
    chunks = near(peers, rows, LANES)

    msg_a, msg_b, cond, leak = pl.pallas_call(
        pack_halo,
        name="pack_halo",
        out_shape=(message, message, slab, slab),
        in_specs=[vmem, vmem, smem, vmem, vmem, vmem, vmem, vmem],
        out_specs=(vmem,) * 4,
    )(permeability, region, region_factor, boundary, pressure_prev, source, concentration, porosity)
    got_a, got_b = exchange(msg_a, msg_b)
    packed = pl.pallas_call(
        pack_flux, name="pack_flux", out_shape=chunks, in_specs=[vmem], out_specs=vmem
    )(flux_prev)
    pad = pltpu.VMEM((layers, PAD, width), f32)
    outgoing, prev_e, u_e, z_e, tx, ty, tz = pl.pallas_call(
        pressure_part,
        name="pressure_part",
        out_shape=(chunks, ext, ext, ext, slab, slab, near(layers - 1, rows, width)),
        in_specs=[vmem] * 7,
        out_specs=(vmem,) * 7,
        scratch_shapes=[pad] * 5,
    )(*keep(got_a, got_b, cond, leak, pressure_prev, source, packed))
    arrived = lax.all_to_all(outgoing, AXIS, split_axis=0, concat_axis=0, tiled=True)
    cells = pltpu.VMEM((kinds, layers, PAD, width), f32)
    return pl.pallas_call(
        finish,
        name="finish",
        out_shape=(arr(layers, rows, width), arr(3, layers, rows, width), arr(kinds, layers, rows, width)),
        in_specs=[vmem] * 5 + [smem] + [vmem] * 6,
        out_specs=(vmem,) * 3,
        scratch_shapes=[pltpu.VMEM((LANES, width), f32), pltpu.VMEM((layers, EXT, width), f32), cells, cells]
        + [pad] * 4,
    )(*keep(arrived, got_a, got_b, concentration, porosity), reaction, *keep(prev_e, u_e, z_e, tx, ty, tz))


def solution(mesh):
    in_specs = (
        P("ens", "gx", None),
        P("ens", "gx", None),
        P("ens", "gx", None),
        P("ens", "gx", None),
        P("ens"),
        P("ens", "gx", None),
        P(None, "ens", "gx", None),
        P(None, "ens", "gx", None),
        P("ens", "gx", None),
        P("ens", None),
    )
    out_specs = (P("ens", "gx", None), P(None, "ens", "gx", None), P(None, "ens", "gx", None))
    return jax.shard_map(shards, mesh=mesh, in_specs=in_specs, out_specs=out_specs, check_vma=False)
```

```python
import functools
import math

import jax
import jax.numpy as jnp
from jax import lax
from jax.experimental import pallas as pl
from jax.experimental.pallas import tpu as pltpu
from jax.sharding import PartitionSpec as P

step_size = 0.5
LANES = 128
WIDE = 3
MID = 2
EXT = 16
PAD = 24
BASE = 1
NEAR_BYTES = 640 * 1024
AXIS = "gx"
PARTS = "ens"


def fits(shape):
    return 4 * math.prod(shape) <= NEAR_BYTES


def odd_device():
    return lax.rem(lax.axis_index(AXIS), 2) == 1


def at_ends():
    index = lax.axis_index(AXIS)
    return index == 0, index == lax.axis_size(AXIS) - 1


def shifted(value, by):
    return pltpu.roll(value, by % value.shape[-1], value.ndim - 1)


def pack_halo(perm, region, rf, boundary, prev, source, conc, por, msg_a, msg_b, cond, leak):
    layers, rows, _ = perm.shape
    kinds = conc.shape[0]
    for z in range(layers):
        factor = jnp.zeros_like(perm[z])
        for r in range(rf.shape[0]):
            factor = jnp.where(region[z] == r, rf[r], factor)
        value = factor * perm[z]
        kind = boundary[z]
        cond[z] = value
        leak[z] = jnp.where(kind == 0, 0.05, jnp.where(kind == 1, 1.0, 10.0)) * value

    def fill(msg, low):
        wide = slice(0, WIDE) if low else slice(rows - WIDE, rows)
        mid = slice(0, MID) if low else slice(rows - MID, rows)
        one = slice(0, 1) if low else slice(rows - 1, rows)
        for z in range(layers):
            row = z * message_rows(kinds)
            for field, part in ((cond, wide), (prev, wide), (source, mid), (leak, mid), (por, one)):
                count = part.stop - part.start
                msg[row : row + count] = field[z, part]
                row += count
            for s in range(kinds):
                msg[row : row + MID] = conc[s, z, mid]
                row += MID

    odd = odd_device()

    @pl.when(odd)
    def _():
        fill(msg_a, True)
        fill(msg_b, False)

    @pl.when(jnp.logical_not(odd))
    def _():
        fill(msg_a, False)
        fill(msg_b, True)


def message_rows(kinds):
    return 2 * WIDE + 2 * MID + 1 + kinds * MID


def pack_flux(flux, reaction, out, rates):
    layers, rows, width = flux.shape[1:]
    groups = LANES // rows
    spot = lax.rem(lax.broadcasted_iota(jnp.int32, (rows, width), 1), rows)
    block = lax.broadcasted_iota(jnp.int32, (rows, LANES), 1) // rows
    tall = [flux[c, z] for c in range(3) for z in range(layers)]
    for z in range(layers):
        along_x, along_y, along_z = flux[0, z], flux[1, z], flux[2, z]
        part = jnp.where(spot <= 1, shifted(along_y, 2), jnp.zeros_like(along_y))
        part = jnp.where(spot == 2, shifted(along_y, -(rows - 2)), part)
        part = jnp.where(spot == 3, shifted(along_x, 4), part)
        part = jnp.where(spot == 4, shifted(along_x, -(rows - 4)), part)
        part = jnp.where(spot == 5, shifted(along_z, 6), part)
        part = jnp.where(spot == 6, shifted(along_z, -(rows - 6)), part)
        tall.append(part)
    for m in range(width // LANES):
        v = [t[:, m * LANES : (m + 1) * LANES] for t in tall]
        d = 1
        while d < groups:
            keep = (block // d) % 2 == 0
            for g in range(groups):
                if g & d == 0:
                    a, b = v[g], v[g + d]
                    v[g] = jnp.where(keep, a, shifted(b, rows * d))
                    v[g + d] = jnp.where(keep, shifted(a, -rows * d), b)
            d *= 2
        for g in range(groups):
            out[m * groups + g] = v[g]
    kinds = reaction.shape[0]
    for s in range(kinds):
        for t in range(kinds):
            rates[s * kinds + t] = jnp.full((rows, width), step_size * reaction[s, t])


def harmonic(left_val, right_val):
    total = left_val + right_val
    return 2.0 * left_val * right_val / jnp.where(total > 0.0, total, 1.0)


def pressure_part(
    kinds, msg_a, msg_b, cond, leak, prev, source, packed, out, prev_e, u_e, z_e, tx_o, ty_o, tz_o, c_s, p_s, s_s, l_s, t_s
):
    layers, rows, width = cond.shape
    top = BASE + WIDE
    end = top + rows
    odd = odd_device()
    zeros = jnp.zeros((PAD, width), jnp.float32)
    is_first, is_last = at_ends()
    for z in range(layers):
        row = z * message_rows(kinds)
        for buf, core, w in ((c_s, cond, WIDE), (p_s, prev, WIDE), (s_s, source, MID), (l_s, leak, MID)):
            first, second = msg_a[row : row + w], msg_b[row : row + w]
            row += w
            buf[z] = zeros
            buf[z, top - w : top] = jnp.where(is_first, 0.0, jnp.where(odd, first, second))
            buf[z, top:end] = core[z]
            buf[z, end : end + w] = jnp.where(is_last, 0.0, jnp.where(odd, second, first))
        t_s[z] = zeros

    here, up, down = pl.ds(BASE, EXT), pl.ds(BASE + 1, EXT), pl.ds(BASE - 1, EXT)
    lane = lax.broadcasted_iota(jnp.int32, (EXT, width), 1)
    upper_x, lower_x, upper_y, lower_y, upper_z, diagonal = [], [], [], [], [], []
    for z in range(layers):
        c = c_s[z, here]
        tx = harmonic(c, c_s[z, up])
        t_s[z, here] = tx
        ty = jnp.where(lane == width - 1, 0.0, harmonic(c, shifted(c, -1)))
        upper_x.append(tx)
        upper_y.append(ty)
        lower_y.append(shifted(ty, 1))
        upper_z.append(harmonic(c, c_s[z + 1, here]) if z + 1 < layers else None)
    for z in range(layers):
        lower_x.append(t_s[z, down])
        diag = l_s[z, here] + lower_x[z] + upper_x[z] + lower_y[z] + upper_y[z]
        if z > 0:
            diag = diag + upper_z[z - 1]
        if z + 1 < layers:
            diag = diag + upper_z[z]
        diagonal.append(diag)

    def around(buf):
        found = []
        for z in range(layers):
            v = buf[z, here]
            total = lower_x[z] * buf[z, down] + upper_x[z] * buf[z, up]
            total = total + lower_y[z] * shifted(v, 1) + upper_y[z] * shifted(v, -1)
            if z > 0:
                total = total + upper_z[z - 1] * buf[z - 1, here]
            if z + 1 < layers:
                total = total + upper_z[z] * buf[z + 1, here]
            found.append(total)
        return found

    inverse = [1.0 / jnp.where(d > 0.0, d, 1.0) for d in diagonal]
    from_prev = around(p_s)
    residual, u = [], []
    for z in range(layers):
        r = s_s[z, here] - (diagonal[z] * p_s[z, here] - from_prev[z])
        residual.append(r)
        u.append(r * inverse[z])
    for z in range(layers):
        s_s[z, here] = u[z]
    from_u = around(s_s)
    zed = [from_u[z] * inverse[z] for z in range(layers)]
    for z in range(layers):
        l_s[z] = zeros
        l_s[z, here] = zed[z]
    from_z = around(l_s)
    core_row = lax.broadcasted_iota(jnp.int32, (EXT, width), 0)
    inside = jnp.logical_and(core_row >= WIDE, core_row < WIDE + rows)

    def total_of(left, right):
        total = left[0] * right[0]
        for z in range(1, layers):
            total = total + left[z] * right[z]
        total = jnp.where(inside, total, 0.0)
        return jnp.sum(jnp.sum(total, axis=0, keepdims=True), axis=1, keepdims=True)

    sums = (total_of(residual, u), total_of(u, from_u), total_of(zed, from_u), total_of(zed, from_z))
    col = lax.broadcasted_iota(jnp.int32, (rows, LANES), 1)
    slots = col < 0
    value = jnp.zeros((rows, LANES), jnp.float32)
    for m, total in enumerate(sums):
        slot = col == (3 * layers + m) * rows + rows - 1
        slots = jnp.logical_or(slots, slot)
        value = jnp.where(slot, total, value)
    for k in range(packed.shape[0]):
        out[k] = jnp.where(slots, value, packed[k])
    for z in range(layers):
        prev_e[z] = p_s[z, here]
        u_e[z] = u[z]
        z_e[z] = zed[z]
        tx_o[z] = t_s[z, top:end]
        ty_o[z] = upper_y[z][WIDE : WIDE + rows]
        if z + 1 < layers:
            tz_o[z] = upper_z[z][WIDE : WIDE + rows]


def prepare(
    msg_a, msg_b, conc, por, rates, prev_e, u_e, z_e, tx, ty, tz, linear, now, local, scale
):
    kinds, layers, rows, width = conc.shape
    for i, field in enumerate((prev_e, u_e, z_e)):
        for z in range(layers):
            p = field[z, WIDE : WIDE + rows]
            linear[i, 0, z] = p
            linear[i, 1, z] = tx[z] * (p - field[z, WIDE + 1 : WIDE + 1 + rows])
            linear[i, 2, z] = ty[z] * (p - shifted(p, -1))
            if z + 1 < layers:
                linear[i, 3, z] = tz[z] * (p - field[z + 1, WIDE : WIDE + rows])
            else:
                linear[i, 3, z] = jnp.zeros_like(p)
    odd = odd_device()
    top = BASE + MID
    end = top + rows
    here = pl.ds(BASE, EXT)
    for z in range(layers):
        row = z * message_rows(kinds) + 2 * WIDE + 2 * MID
        first, second = msg_a[row : row + 1], msg_b[row : row + 1]
        scale[z] = jnp.ones((EXT, width), jnp.float32)
        scale[z, MID - 1 : MID] = jnp.where(odd, first, second)
        scale[z, MID : MID + rows] = por[z]
        scale[z, MID + rows : MID + rows + 1] = jnp.where(odd, second, first)
        row += 1
        for s in range(kinds):
            first, second = msg_a[row : row + MID], msg_b[row : row + MID]
            now[s, z] = jnp.zeros((PAD, width), jnp.float32)
            now[s, z, top - MID : top] = jnp.where(odd, first, second)
            now[s, z, top:end] = conc[s, z]
            now[s, z, end : end + MID] = jnp.where(odd, second, first)
            row += MID
    for z in range(layers):
        scale[z] = step_size / scale[z]
        cells = [now[s, z, here] for s in range(kinds)]
        for s in range(kinds):
            total = cells[s]
            for t in range(kinds):
                rate = rates[s * kinds + t]
                total = total + jnp.concatenate([rate] * (EXT // rows), axis=0) * cells[t]
            local[s, z] = total


def finish(
    arrived, linear, now, local, scale, rates, pressure, flux_new, species, turned, later, fx_s, fy_s, fz_s
):
    kinds, layers = now.shape[:2]
    rows, width = arrived.shape[1], now.shape[-1]
    turned[...] = jnp.transpose(arrived[...].reshape(width, LANES))
    halo = 3 * layers * rows

    sums = [
        jnp.sum(turned[halo + rows * m + rows - 1 : halo + rows * (m + 1), :], axis=1, keepdims=True) * (1.0 / rows)
        for m in range(4)
    ]
    g, h, k, l = sums
    first = g / (g - h)
    rest = 1.0 - first
    gamma = rest * rest * g + 2.0 * first * rest * h + first * first * k
    weight = rest + gamma / g
    bend = weight * weight * (g - h) + 2.0 * weight * first * (h - k) + first * first * (k - l)
    second = gamma / bend
    of_u = first + second * weight
    of_z = second * first
    for z in range(layers):
        for i in range(4):
            value = linear[0, i, z] + of_u * linear[1, i, z] + of_z * linear[2, i, z]
            if i == 0:
                pressure[z] = value
            else:
                flux_new[i - 1, z] = value

    is_first, is_last = at_ends()
    top = BASE + MID
    end = top + rows
    last_row = lax.broadcasted_iota(jnp.int32, (rows, width), 0) == rows - 1
    closed = jnp.logical_and(is_last, last_row)
    for z in range(layers):
        for buf, c in ((fx_s, 0), (fy_s, 1), (fz_s, 2)):
            group = (c * layers + z) * rows
            block = turned[group : group + rows, :]
            buf[z, 0:8] = jnp.zeros((8, width), jnp.float32)
            buf[z, PAD - 16 : PAD - 8] = jnp.zeros((8, width), jnp.float32)
            buf[z, PAD - 8 : PAD] = jnp.zeros((8, width), jnp.float32)
            buf[z, top:end] = jnp.where(closed, 0.0, block) if c == 1 else block
        extra = halo + rows * z
        fy_s[z, top - 2 : top - 1] = turned[extra : extra + 1, :]
        fy_s[z, top - 1 : top] = jnp.where(is_first, 0.0, turned[extra + 1 : extra + 2, :])
        fy_s[z, end : end + 1] = turned[extra + 2 : extra + 3, :]
        fx_s[z, top - 1 : top] = turned[extra + 3 : extra + 4, :]
        fx_s[z, end : end + 1] = turned[extra + 4 : extra + 5, :]
        fz_s[z, top - 1 : top] = turned[extra + 5 : extra + 6, :]
        fz_s[z, end : end + 1] = turned[extra + 6 : extra + 7, :]

    def weights(start, count):
        lane = lax.broadcasted_iota(jnp.int32, (count, width), 1)
        here, down = pl.ds(start, count), pl.ds(start - 1, count)
        found = []
        fz_low = None
        for z in range(layers):
            pores = scale[z, start - BASE : start - BASE + count]
            fy, fy_low = fy_s[z, here], fy_s[z, down]
            fx = jnp.where(lane == width - 1, 0.0, fx_s[z, here])
            out_x, in_x = jnp.maximum(fx, 0.0), jnp.minimum(fx, 0.0)
            low_out, low_in = shifted(out_x, 1), shifted(in_x, 1)
            centre = jnp.minimum(fy_low, 0.0) - jnp.maximum(fy, 0.0) - out_x + low_in
            y_up, y_down = -pores * jnp.minimum(fy, 0.0), pores * jnp.maximum(fy_low, 0.0)
            x_up, x_down = -pores * in_x, pores * low_out
            z_up = z_down = None
            if z > 0:
                centre = centre + jnp.minimum(fz_low, 0.0)
                z_down = pores * jnp.maximum(fz_low, 0.0)
            if z + 1 < layers:
                fz = fz_s[z, here]
                centre = centre - jnp.maximum(fz, 0.0)
                z_up = -pores * jnp.minimum(fz, 0.0)
                fz_low = fz
            found.append((pores * centre, y_up, y_down, x_up, x_down, z_up, z_down))
        return found

    def advance(buf, rest, put, start, count):
        here, up, down = pl.ds(start, count), pl.ds(start + 1, count), pl.ds(start - 1, count)
        coefficients = weights(start, count)
        for z in range(layers):
            centre, y_up, y_down, x_up, x_down, z_up, z_down = coefficients[z]
            cells = [buf[s, z, here] for s in range(kinds)]
            for s in range(kinds):
                v = cells[s]
                total = rest(s, z, cells) + centre * v
                total = total + y_up * buf[s, z, up] + y_down * buf[s, z, down]
                total = total + x_up * shifted(v, -1) + x_down * shifted(v, 1)
                if z > 0:
                    total = total + z_down * buf[s, z - 1, here]
                if z + 1 < layers:
                    total = total + z_up * buf[s, z + 1, here]
                put(s, z, total)

    def put_later(s, z, value):
        later[s, z, BASE : BASE + EXT] = value

    def put_out(s, z, value):
        species[s, z] = value

    def reacted(s, z, cells):
        total = cells[s]
        for t in range(kinds):
            total = total + rates[s * kinds + t] * cells[t]
        return total

    advance(now, lambda s, z, cells: local[s, z], put_later, BASE, EXT)
    advance(later, reacted, put_out, top, rows)


def exchange(msg_a, msg_b):
    peers, parts = lax.axis_size(AXIS), lax.axis_size(PARTS)
    assert peers % 2 == 0
    partner = [(i, i + 1) for i in range(0, peers, 2)]
    other = [(i, i + 1) for i in range(1, peers - 1, 2)]
    pairs = [(e * peers + i, e * peers + j) for e in range(parts) for i, j in other]
    pairs += [(e * peers + i, (e + 1) * peers + i) for e in range(0, parts - 1, 2) for i in (0, peers - 1)]
    got_a = lax.ppermute(msg_a, AXIS, partner + [(j, i) for i, j in partner])
    got_b = lax.ppermute(msg_b, (PARTS, AXIS), pairs + [(j, i) for i, j in pairs])
    return got_a, got_b


def shards(
    pressure_prev, source, permeability, region, region_factor, boundary, flux_prev, concentration, porosity, reaction
):
    layers, rows, width = permeability.shape
    kinds = concentration.shape[0]
    peers = lax.axis_size(AXIS)
    assert rows * peers == width and concentration.shape[-1] == width
    assert rows == 8 and 4 * layers * rows == LANES and layers >= 4 and 2 * kinds <= rows
    f32 = jnp.float32
    vmem = pl.BlockSpec(memory_space=pltpu.VMEM)
    smem = pl.BlockSpec(memory_space=pltpu.SMEM)

    def arr(*shape):
        return jax.ShapeDtypeStruct(shape, f32)

    def near(*shape):
        return pltpu.VMEM(shape, f32) if fits(shape) else arr(*shape)

    def keep(*arrays):
        return [pltpu.with_memory_space_constraint(a, pltpu.VMEM) if fits(a.shape) else a for a in arrays]

    message = near(-(-layers * message_rows(kinds) // 8) * 8, width)
    slab = near(layers, rows, width)
    ext = near(layers, EXT, width)
    chunks = near(peers, rows, LANES)
    cells = near(kinds, layers, PAD, width)
    rate = near(kinds * kinds, rows, width)

    msg_a, msg_b, cond, leak = pl.pallas_call(
        pack_halo,
        name="pack_halo",
        out_shape=(message, message, slab, slab),
        in_specs=[vmem, vmem, smem, vmem, vmem, vmem, vmem, vmem],
        out_specs=(vmem,) * 4,
    )(permeability, region, region_factor, boundary, pressure_prev, source, concentration, porosity)
    got_a, got_b = exchange(msg_a, msg_b)
    packed, rates = pl.pallas_call(
        pack_flux, name="pack_flux", out_shape=(chunks, rate), in_specs=[vmem, smem], out_specs=(vmem, vmem)
    )(flux_prev, reaction)
    pad = pltpu.VMEM((layers, PAD, width), f32)
    outgoing, *fields = pl.pallas_call(
        functools.partial(pressure_part, kinds),
        name="pressure_part",
        out_shape=(chunks, ext, ext, ext, slab, slab, near(layers - 1, rows, width)),
        in_specs=[vmem] * 7,
        out_specs=(vmem,) * 7,
        scratch_shapes=[pad] * 5,
    )(*keep(got_a, got_b, cond, leak, pressure_prev, source, packed))
    arrived = lax.all_to_all(outgoing, AXIS, split_axis=0, concat_axis=0, tiled=True)
    linear, now, local, scale = pl.pallas_call(
        prepare,
        name="prepare",
        out_shape=(near(3, 4, layers, rows, width), cells, near(kinds, layers, EXT, width), ext),
        in_specs=[vmem] * 11,
        out_specs=(vmem,) * 4,
    )(*keep(got_a, got_b, concentration, porosity, rates, *fields))
    return pl.pallas_call(
        finish,
        name="finish",
        out_shape=(arr(layers, rows, width), arr(3, layers, rows, width), arr(kinds, layers, rows, width)),
        in_specs=[vmem] * 6,
        out_specs=(vmem,) * 3,
        scratch_shapes=[pltpu.VMEM((LANES, width), f32), pltpu.VMEM((kinds, layers, PAD, width), f32)] + [pad] * 3,
    )(*keep(arrived, linear, now, local, scale, rates))


def solution(mesh):
    in_specs = (
        P("ens", "gx", None),
        P("ens", "gx", None),
        P("ens", "gx", None),
        P("ens", "gx", None),
        P("ens"),
        P("ens", "gx", None),
        P(None, "ens", "gx", None),
        P(None, "ens", "gx", None),
        P("ens", "gx", None),
        P("ens", None),
    )
    out_specs = (P("ens", "gx", None), P(None, "ens", "gx", None), P(None, "ens", "gx", None))
    return jax.shard_map(shards, mesh=mesh, in_specs=in_specs, out_specs=out_specs, check_vma=False)
```

```python
import functools
import math

import jax
import jax.numpy as jnp
from jax import lax
from jax.experimental import pallas as pl
from jax.experimental.pallas import tpu as pltpu
from jax.sharding import PartitionSpec as P

step_size = 0.5
LANES = 128
WIDE = 3
MID = 2
EXT = 16
PAD = 24
BASE = 1
NEAR_BYTES = 640 * 1024
AXIS = "gx"
PARTS = "ens"


def fits(shape):
    return 4 * math.prod(shape) <= NEAR_BYTES


def odd_device():
    return lax.rem(lax.axis_index(AXIS), 2) == 1


def at_ends():
    index = lax.axis_index(AXIS)
    return index == 0, index == lax.axis_size(AXIS) - 1


def shifted(value, by):
    return pltpu.roll(value, by % value.shape[-1], value.ndim - 1)


def pack_halo(perm, region, rf, boundary, prev, source, conc, por, msg_a, msg_b, cond, leak):
    layers, rows, _ = perm.shape
    kinds = conc.shape[0]
    for z in range(layers):
        factor = jnp.zeros_like(perm[z])
        for r in range(rf.shape[0]):
            factor = jnp.where(region[z] == r, rf[r], factor)
        value = factor * perm[z]
        kind = boundary[z]
        cond[z] = value
        leak[z] = jnp.where(kind == 0, 0.05, jnp.where(kind == 1, 1.0, 10.0)) * value

    def fill(msg, low):
        wide = slice(0, WIDE) if low else slice(rows - WIDE, rows)
        mid = slice(0, MID) if low else slice(rows - MID, rows)
        one = slice(0, 1) if low else slice(rows - 1, rows)
        for z in range(layers):
            row = z * message_rows(kinds)
            for field, part in ((cond, wide), (prev, wide), (source, mid), (leak, mid), (por, one)):
                count = part.stop - part.start
                msg[row : row + count] = field[z, part]
                row += count
            for s in range(kinds):
                msg[row : row + MID] = conc[s, z, mid]
                row += MID

    odd = odd_device()

    @pl.when(odd)
    def _():
        fill(msg_a, True)
        fill(msg_b, False)

    @pl.when(jnp.logical_not(odd))
    def _():
        fill(msg_a, False)
        fill(msg_b, True)


def message_rows(kinds):
    return 2 * WIDE + 2 * MID + 1 + kinds * MID


def pack_flux(flux, reaction, out, rates):
    layers, rows, width = flux.shape[1:]
    groups = LANES // rows
    spot = lax.rem(lax.broadcasted_iota(jnp.int32, (rows, width), 1), rows)
    block = lax.broadcasted_iota(jnp.int32, (rows, LANES), 1) // rows
    tall = [flux[c, z] for c in range(3) for z in range(layers)]
    for z in range(layers):
        along_x, along_y, along_z = flux[0, z], flux[1, z], flux[2, z]
        part = jnp.where(spot <= 1, shifted(along_y, 2), jnp.zeros_like(along_y))
        part = jnp.where(spot == 2, shifted(along_y, -(rows - 2)), part)
        part = jnp.where(spot == 3, shifted(along_x, 4), part)
        part = jnp.where(spot == 4, shifted(along_x, -(rows - 4)), part)
        part = jnp.where(spot == 5, shifted(along_z, 6), part)
        part = jnp.where(spot == 6, shifted(along_z, -(rows - 6)), part)
        tall.append(part)
    for m in range(width // LANES):
        v = [t[:, m * LANES : (m + 1) * LANES] for t in tall]
        d = 1
        while d < groups:
            keep = (block // d) % 2 == 0
            for g in range(groups):
                if g & d == 0:
                    a, b = v[g], v[g + d]
                    v[g] = jnp.where(keep, a, shifted(b, rows * d))
                    v[g + d] = jnp.where(keep, shifted(a, -rows * d), b)
            d *= 2
        for g in range(groups):
            out[m * groups + g] = v[g]
    kinds = reaction.shape[0]
    for s in range(kinds):
        for t in range(kinds):
            rates[s * kinds + t] = jnp.full((rows, width), step_size * reaction[s, t])


def harmonic(left_val, right_val):
    total = left_val + right_val
    return 2.0 * left_val * right_val / jnp.where(total > 0.0, total, 1.0)


def pressure_part(
    kinds, msg_a, msg_b, cond, leak, prev, source, packed, out, prev_e, u_e, z_e, tx_o, ty_o, tz_o, c_s, p_s, s_s, l_s, t_s
):
    layers, rows, width = cond.shape
    top = BASE + WIDE
    end = top + rows
    odd = odd_device()
    zeros = jnp.zeros((PAD, width), jnp.float32)
    is_first, is_last = at_ends()
    for z in range(layers):
        row = z * message_rows(kinds)
        for buf, core, w in ((c_s, cond, WIDE), (p_s, prev, WIDE), (s_s, source, MID), (l_s, leak, MID)):
            first, second = msg_a[row : row + w], msg_b[row : row + w]
            row += w
            buf[z] = zeros
            buf[z, top - w : top] = jnp.where(is_first, 0.0, jnp.where(odd, first, second))
            buf[z, top:end] = core[z]
            buf[z, end : end + w] = jnp.where(is_last, 0.0, jnp.where(odd, second, first))
        t_s[z] = zeros

    here, up, down = pl.ds(BASE, EXT), pl.ds(BASE + 1, EXT), pl.ds(BASE - 1, EXT)
    lane = lax.broadcasted_iota(jnp.int32, (EXT, width), 1)
    upper_x, lower_x, upper_y, lower_y, upper_z, diagonal = [], [], [], [], [], []
    for z in range(layers):
        c = c_s[z, here]
        tx = harmonic(c, c_s[z, up])
        t_s[z, here] = tx
        ty = jnp.where(lane == width - 1, 0.0, harmonic(c, shifted(c, -1)))
        upper_x.append(tx)
        upper_y.append(ty)
        lower_y.append(shifted(ty, 1))
        upper_z.append(harmonic(c, c_s[z + 1, here]) if z + 1 < layers else None)
    for z in range(layers):
        lower_x.append(t_s[z, down])
        diag = l_s[z, here] + lower_x[z] + upper_x[z] + lower_y[z] + upper_y[z]
        if z > 0:
            diag = diag + upper_z[z - 1]
        if z + 1 < layers:
            diag = diag + upper_z[z]
        diagonal.append(diag)

    def around(buf):
        found = []
        for z in range(layers):
            v = buf[z, here]
            total = lower_x[z] * buf[z, down] + upper_x[z] * buf[z, up]
            total = total + lower_y[z] * shifted(v, 1) + upper_y[z] * shifted(v, -1)
            if z > 0:
                total = total + upper_z[z - 1] * buf[z - 1, here]
            if z + 1 < layers:
                total = total + upper_z[z] * buf[z + 1, here]
            found.append(total)
        return found

    inverse = [1.0 / jnp.where(d > 0.0, d, 1.0) for d in diagonal]
    from_prev = around(p_s)
    residual, u = [], []
    for z in range(layers):
        r = s_s[z, here] - (diagonal[z] * p_s[z, here] - from_prev[z])
        residual.append(r)
        u.append(r * inverse[z])
    for z in range(layers):
        s_s[z, here] = u[z]
    from_u = around(s_s)
    zed = [from_u[z] * inverse[z] for z in range(layers)]
    for z in range(layers):
        l_s[z] = zeros
        l_s[z, here] = zed[z]
    from_z = around(l_s)
    core_row = lax.broadcasted_iota(jnp.int32, (EXT, width), 0)
    inside = jnp.logical_and(core_row >= WIDE, core_row < WIDE + rows)

    def total_of(left, right):
        total = left[0] * right[0]
        for z in range(1, layers):
            total = total + left[z] * right[z]
        total = jnp.where(inside, total, 0.0)
        return jnp.sum(jnp.sum(total, axis=0, keepdims=True), axis=1, keepdims=True)

    sums = (total_of(residual, u), total_of(u, from_u), total_of(zed, from_u), total_of(zed, from_z))
    col = lax.broadcasted_iota(jnp.int32, (rows, LANES), 1)
    slots = col < 0
    value = jnp.zeros((rows, LANES), jnp.float32)
    for m, total in enumerate(sums):
        slot = col == (3 * layers + m) * rows + rows - 1
        slots = jnp.logical_or(slots, slot)
        value = jnp.where(slot, total, value)
    for k in range(packed.shape[0]):
        out[k] = jnp.where(slots, value, packed[k])
    for z in range(layers):
        prev_e[z] = p_s[z, here]
        u_e[z] = u[z]
        z_e[z] = zed[z]
        tx_o[z] = t_s[z, top:end]
        ty_o[z] = upper_y[z][WIDE : WIDE + rows]
        if z + 1 < layers:
            tz_o[z] = upper_z[z][WIDE : WIDE + rows]


def finish(
    arrived, msg_a, msg_b, conc, por, rates, prev_e, u_e, z_e, tx, ty, tz,
    pressure, flux_new, species, turned, p_s, now, later, local, scale, fx_s, fy_s, fz_s,
):
    kinds, layers, rows, width = conc.shape
    turned[...] = jnp.transpose(arrived[...].reshape(width, LANES))
    halo = 3 * layers * rows

    odd = odd_device()
    top = BASE + MID
    end = top + rows
    for z in range(layers):
        row = z * message_rows(kinds) + 2 * WIDE + 2 * MID
        first, second = msg_a[row : row + 1], msg_b[row : row + 1]
        scale[z] = jnp.ones((EXT, width), jnp.float32)
        scale[z, MID - 1 : MID] = jnp.where(odd, first, second)
        scale[z, MID : MID + rows] = por[z]
        scale[z, MID + rows : MID + rows + 1] = jnp.where(odd, second, first)
        row += 1
        for s in range(kinds):
            first, second = msg_a[row : row + MID], msg_b[row : row + MID]
            now[s, z] = jnp.zeros((PAD, width), jnp.float32)
            now[s, z, top - MID : top] = jnp.where(odd, first, second)
            now[s, z, top:end] = conc[s, z]
            now[s, z, end : end + MID] = jnp.where(odd, second, first)
            row += MID
    for z in range(layers):
        scale[z] = step_size / scale[z]
        cells = [now[s, z, pl.ds(BASE, EXT)] for s in range(kinds)]
        for s in range(kinds):
            total = cells[s]
            for t in range(kinds):
                rate = rates[s * kinds + t]
                total = total + jnp.concatenate([rate] * (EXT // rows), axis=0) * cells[t]
            local[s, z] = total

    sums = [
        jnp.sum(turned[halo + rows * m + rows - 1 : halo + rows * (m + 1), :], axis=1, keepdims=True) * (1.0 / rows)
        for m in range(4)
    ]
    g, h, k, l = sums
    first = g / (g - h)
    rest = 1.0 - first
    gamma = rest * rest * g + 2.0 * first * rest * h + first * first * k
    weight = rest + gamma / g
    bend = weight * weight * (g - h) + 2.0 * weight * first * (h - k) + first * first * (k - l)
    second = gamma / bend
    of_u = first + second * weight
    of_z = second * first
    for z in range(layers):
        p_s[z] = prev_e[z] + of_u * u_e[z] + of_z * z_e[z]
    for z in range(layers):
        p = p_s[z, WIDE : WIDE + rows]
        pressure[z] = p
        flux_new[0, z] = tx[z] * (p - p_s[z, WIDE + 1 : WIDE + 1 + rows])
        flux_new[1, z] = ty[z] * (p - shifted(p, -1))
        if z + 1 < layers:
            flux_new[2, z] = tz[z] * (p - p_s[z + 1, WIDE : WIDE + rows])
        else:
            flux_new[2, z] = jnp.zeros_like(p)

    is_first, is_last = at_ends()
    last_row = lax.broadcasted_iota(jnp.int32, (rows, width), 0) == rows - 1
    closed = jnp.logical_and(is_last, last_row)
    for z in range(layers):
        for buf, c in ((fx_s, 0), (fy_s, 1), (fz_s, 2)):
            group = (c * layers + z) * rows
            block = turned[group : group + rows, :]
            buf[z, 0:8] = jnp.zeros((8, width), jnp.float32)
            buf[z, PAD - 16 : PAD - 8] = jnp.zeros((8, width), jnp.float32)
            buf[z, PAD - 8 : PAD] = jnp.zeros((8, width), jnp.float32)
            buf[z, top:end] = jnp.where(closed, 0.0, block) if c == 1 else block
        extra = halo + rows * z
        fy_s[z, top - 2 : top - 1] = turned[extra : extra + 1, :]
        fy_s[z, top - 1 : top] = jnp.where(is_first, 0.0, turned[extra + 1 : extra + 2, :])
        fy_s[z, end : end + 1] = turned[extra + 2 : extra + 3, :]
        fx_s[z, top - 1 : top] = turned[extra + 3 : extra + 4, :]
        fx_s[z, end : end + 1] = turned[extra + 4 : extra + 5, :]
        fz_s[z, top - 1 : top] = turned[extra + 5 : extra + 6, :]
        fz_s[z, end : end + 1] = turned[extra + 6 : extra + 7, :]

    def weights(start, count):
        lane = lax.broadcasted_iota(jnp.int32, (count, width), 1)
        here, down = pl.ds(start, count), pl.ds(start - 1, count)
        found = []
        fz_low = None
        for z in range(layers):
            pores = scale[z, start - BASE : start - BASE + count]
            fy, fy_low = fy_s[z, here], fy_s[z, down]
            fx = jnp.where(lane == width - 1, 0.0, fx_s[z, here])
            out_x, in_x = jnp.maximum(fx, 0.0), jnp.minimum(fx, 0.0)
            low_out, low_in = shifted(out_x, 1), shifted(in_x, 1)
            centre = jnp.minimum(fy_low, 0.0) - jnp.maximum(fy, 0.0) - out_x + low_in
            y_up, y_down = -pores * jnp.minimum(fy, 0.0), pores * jnp.maximum(fy_low, 0.0)
            x_up, x_down = -pores * in_x, pores * low_out
            z_up = z_down = None
            if z > 0:
                centre = centre + jnp.minimum(fz_low, 0.0)
                z_down = pores * jnp.maximum(fz_low, 0.0)
            if z + 1 < layers:
                fz = fz_s[z, here]
                centre = centre - jnp.maximum(fz, 0.0)
                z_up = -pores * jnp.minimum(fz, 0.0)
                fz_low = fz
            found.append((pores * centre, y_up, y_down, x_up, x_down, z_up, z_down))
        return found

    def advance(buf, rest, put, start, count):
        here, up, down = pl.ds(start, count), pl.ds(start + 1, count), pl.ds(start - 1, count)
        coefficients = weights(start, count)
        for z in range(layers):
            centre, y_up, y_down, x_up, x_down, z_up, z_down = coefficients[z]
            cells = [buf[s, z, here] for s in range(kinds)]
            for s in range(kinds):
                v = cells[s]
                total = rest(s, z, cells) + centre * v
                total = total + y_up * buf[s, z, up] + y_down * buf[s, z, down]
                total = total + x_up * shifted(v, -1) + x_down * shifted(v, 1)
                if z > 0:
                    total = total + z_down * buf[s, z - 1, here]
                if z + 1 < layers:
                    total = total + z_up * buf[s, z + 1, here]
                put(s, z, total)

    def put_later(s, z, value):
        later[s, z, BASE : BASE + EXT] = value

    def put_out(s, z, value):
        species[s, z] = value

    def reacted(s, z, cells):
        total = cells[s]
        for t in range(kinds):
            total = total + rates[s * kinds + t] * cells[t]
        return total

    advance(now, lambda s, z, cells: local[s, z], put_later, BASE, EXT)
    advance(later, reacted, put_out, top, rows)


def exchange(msg_a, msg_b):
    peers, parts = lax.axis_size(AXIS), lax.axis_size(PARTS)
    assert peers % 2 == 0
    partner = [(i, i + 1) for i in range(0, peers, 2)]
    other = [(i, i + 1) for i in range(1, peers - 1, 2)]
    pairs = [(e * peers + i, e * peers + j) for e in range(parts) for i, j in other]
    pairs += [(e * peers + i, (e + 1) * peers + i) for e in range(0, parts - 1, 2) for i in (0, peers - 1)]
    got_a = lax.ppermute(msg_a, AXIS, partner + [(j, i) for i, j in partner])
    got_b = lax.ppermute(msg_b, (PARTS, AXIS), pairs + [(j, i) for i, j in pairs])
    return got_a, got_b


def shards(
    pressure_prev, source, permeability, region, region_factor, boundary, flux_prev, concentration, porosity, reaction
):
    layers, rows, width = permeability.shape
    kinds = concentration.shape[0]
    peers = lax.axis_size(AXIS)
    assert rows * peers == width and concentration.shape[-1] == width
    assert rows == 8 and 4 * layers * rows == LANES and layers >= 4 and 2 * kinds <= rows
    f32 = jnp.float32
    vmem = pl.BlockSpec(memory_space=pltpu.VMEM)
    smem = pl.BlockSpec(memory_space=pltpu.SMEM)

    def arr(*shape):
        return jax.ShapeDtypeStruct(shape, f32)

    def near(*shape):
        return pltpu.VMEM(shape, f32) if fits(shape) else arr(*shape)

    def keep(*arrays):
        return [pltpu.with_memory_space_constraint(a, pltpu.VMEM) if fits(a.shape) else a for a in arrays]

    message = near(-(-layers * message_rows(kinds) // 8) * 8, width)
    slab = near(layers, rows, width)
    ext = near(layers, EXT, width)
    chunks = near(peers, rows, LANES)
    rate = near(kinds * kinds, rows, width)

    msg_a, msg_b, cond, leak = pl.pallas_call(
        pack_halo,
        name="pack_halo",
        out_shape=(message, message, slab, slab),
        in_specs=[vmem, vmem, smem, vmem, vmem, vmem, vmem, vmem],
        out_specs=(vmem,) * 4,
    )(permeability, region, region_factor, boundary, pressure_prev, source, concentration, porosity)
    got_a, got_b = exchange(msg_a, msg_b)
    packed, rates = pl.pallas_call(
        pack_flux, name="pack_flux", out_shape=(chunks, rate), in_specs=[vmem, smem], out_specs=(vmem, vmem)
    )(flux_prev, reaction)
    pad = pltpu.VMEM((layers, PAD, width), f32)
    outgoing, *fields = pl.pallas_call(
        functools.partial(pressure_part, kinds),
        name="pressure_part",
        out_shape=(chunks, ext, ext, ext, slab, slab, near(layers - 1, rows, width)),
        in_specs=[vmem] * 7,
        out_specs=(vmem,) * 7,
        scratch_shapes=[pad] * 5,
    )(*keep(got_a, got_b, cond, leak, pressure_prev, source, packed))
    arrived = lax.all_to_all(outgoing, AXIS, split_axis=0, concat_axis=0, tiled=True)
    cells = pltpu.VMEM((kinds, layers, PAD, width), f32)
    extended = pltpu.VMEM((layers, EXT, width), f32)
    return pl.pallas_call(
        finish,
        name="finish",
        out_shape=(arr(layers, rows, width), arr(3, layers, rows, width), arr(kinds, layers, rows, width)),
        in_specs=[vmem] * 12,
        out_specs=(vmem,) * 3,
        scratch_shapes=[pltpu.VMEM((LANES, width), f32), extended, cells, cells]
        + [pltpu.VMEM((kinds, layers, EXT, width), f32), extended, pad, pad, pad],
    )(*keep(arrived, got_a, got_b, concentration, porosity, rates, *fields))


def solution(mesh):
    in_specs = (
        P("ens", "gx", None),
        P("ens", "gx", None),
        P("ens", "gx", None),
        P("ens", "gx", None),
        P("ens"),
        P("ens", "gx", None),
        P(None, "ens", "gx", None),
        P(None, "ens", "gx", None),
        P("ens", "gx", None),
        P("ens", None),
    )
    out_specs = (P("ens", "gx", None), P(None, "ens", "gx", None), P(None, "ens", "gx", None))
    return jax.shard_map(shards, mesh=mesh, in_specs=in_specs, out_specs=out_specs, check_vma=False)
```
